32 devices in a mesh: parts: 1, sens: 32 (over z, y, x, core).
Axes of the slice: x: 2, y: 2, z: 4, core: 2. Of those that a mesh axis runs over, the one named last changes fastest.
Arguments:
- data: bfloat16 [5120, 2048], P(('parts', 'sens'))
- templates: bfloat16 [1024, 16, 256], P('sens')
- cover: int32 [1024, 16], P('sens'), may hold values from 0 to 31, all different within a row; in each aligned block of 32 rows (0 to 31, 32 to 63, ...) at most 20 rows name the same one
- channel: int32 [1024, 16], P('sens'), may hold values from 0 to 63
Outputs:
- stacked: float32 [1024, 4864], P(('parts', 'sens'))
The draws below stay inside these ranges and needn't reach their ends.
Inputs may be any that keep to these rules, and one draw needn't show every extreme that they name: `cover`: each row names 16 different sensor groups. Within the 32 rows of one device no group is named by more than 20 rows, a bound that some of them reach.
All inputs are finite; a program needn't handle non-finite values.
Results may differ from the reference program's by a relative error of at most 0.0003.
Values may be sent and summed in bfloat16 or wider, within the bound.
No kernel may reach another device: no remote copies, remote signals or barrier semaphores. Data moves between devices by JAX's collectives and lax.ppermute only.
A program may use at most 128 MiB of HBM per device.

```python
import math
import jax
import jax.numpy as jnp
import numpy as np
from jax import lax

S = 2048
C = 16
L = 256
TPL_DEV = 32
K = 1024
SG = 64
CAP = 20
TIME = 5120
LAGS = 4864
N_SENS = 32


def draw_data(key, part):
    key_rows = jax.random.fold_in(key, 11)
    key_cols = jax.random.fold_in(key, 12)
    key_noise = jax.random.fold_in(key, 13)
    row_scale = jnp.exp(jax.random.uniform(key_rows, (TIME, 1), jnp.float32, -1.15, 1.15))
    col_scale = jnp.exp(jax.random.uniform(key_cols, (1, S), jnp.float32, -1.15, 1.15))
    noise_field = jax.random.normal(key_noise, (TIME, S), jnp.float32)
    return (noise_field * row_scale * col_scale).astype(jnp.bfloat16)


def draw_templates(key, part):
    key_rows = jax.random.fold_in(key, 21)
    key_fine = jax.random.fold_in(key, 22)
    key_noise = jax.random.fold_in(key, 23)
    row_scale = jnp.exp(jax.random.uniform(key_rows, (K, C, 1), jnp.float32, -1.15, 1.15))
    fine_scale = jnp.exp(jax.random.uniform(key_fine, (K, C, L), jnp.float32, -0.35, 0.35))
    noise_field = jax.random.normal(key_noise, (K, C, L), jnp.float32)
    return (noise_field * row_scale * fine_scale).astype(jnp.bfloat16)


def set_ends(drawn, stream_key, low, high):
    place = [jax.random.randint(jax.random.fold_in(stream_key, axis), (), 0, length) for axis, length in enumerate(drawn.shape)]
    longest = drawn.shape.index(max(drawn.shape))
    beside = place[:longest] + [(place[longest] + 1) % drawn.shape[longest]] + place[longest + 1:]
    return drawn.at[tuple(place)].set(low).at[tuple(beside)].set(high)


def assign_block(key, own, number, rows, count, top, bound, lean):
    sequence = jax.random.permutation(key, count)
    heavy_load, usual = load_shares(count, rows * top, bound, lean, True), load_shares(count, rows * top, bound, lean, False)
    places = jnp.arange(count)

    def named(tallies, turn):
        used = int((tallies > 0).sum())
        fixed = max(1, used // 4)
        moved = fixed + (places - fixed + turn * (used - fixed)) % max(1, count - fixed)
        return jnp.zeros((count,), jnp.int32).at[sequence[jnp.where(places < fixed, places, moved)]].set(jnp.asarray(tallies, jnp.int32))

    tallies = jnp.where(number % 4 == 0, named(heavy_load, number // 4), named(usual, number - number // 4 - 1))
    mixed = jax.random.permutation(jax.random.fold_in(own, 3), count)
    donor, receiver = mixed[0:count // 2 * 2:2], mixed[1:count // 2 * 2:2]
    margin = jnp.minimum(tallies[donor] - 1, bound - tallies[receiver]) // 2
    margin = jnp.where((donor == sequence[0]) | (receiver == sequence[0]) | (tallies[receiver] == 0), 0, jnp.maximum(margin, 0))
    moved = jax.random.randint(jax.random.fold_in(own, 4), (count // 2,), 0, 1 << 20) % (margin + 1)
    tallies = tallies.at[donor].add(-moved).at[receiver].add(moved)
    members = jnp.searchsorted(jnp.cumsum(tallies), jnp.arange(rows * top), side="right").astype(jnp.int32)
    listing = members.reshape(top, rows).T
    listing = listing[jax.random.permutation(jax.random.fold_in(own, 1), rows)]
    turn = jax.random.randint(jax.random.fold_in(own, 2), (rows, 1), 0, top)
    return jnp.take_along_axis(listing, (jnp.arange(top)[None, :] + turn) % top, axis=1)


def load_shares(count, total, bound, slope, full):
    portions = [(1 << 20) // math.isqrt(standing ** slope) + 1 for standing in range(1, count + 1)]
    largest = bound if full else min(bound, max(-(-total // count), total * portions[0] // sum(portions)))
    least = 1 if total - largest >= count - 1 else 0
    given, spare = [largest] + [least] * (count - 1), total - largest - least * (count - 1)
    while spare > 0:
        movable = [i for i in range(1, count) if given[i] < largest] or [i for i in range(1, count) if given[i] < bound]
        mass, remaining = sum([portions[i] for i in movable]), spare
        for i in movable:
            more = min(bound - given[i], max(1, remaining * portions[i] // mass), spare)
            given[i] = given[i] + more
            spare = spare - more
    return np.array(given)


def setup_inputs(seed: int = 0, part: int = 0) -> dict:
    seeds = jax.random.split(jax.random.key(seed), 5)
    part_splits = jax.random.split(jax.random.fold_in(seeds[4], part), 5)
    data = draw_data(jax.random.fold_in(jax.random.fold_in(seeds[4], part), 71), part)
    templates = draw_templates(jax.random.fold_in(seeds[4], 71), part)
    cover_keys = jax.random.split(jax.random.fold_in(seeds[2], 1), K // TPL_DEV)
    cover_turns = jax.random.permutation(jax.random.fold_in(seeds[2], 3), K // TPL_DEV)
    cover = jax.vmap(lambda own, number: assign_block(jax.random.fold_in(seeds[2], 2), own, number, TPL_DEV, N_SENS, C, CAP, 2))(cover_keys, cover_turns).reshape((K, C))
    channel = set_ends(jax.random.randint(seeds[3], (K, C), 0, SG), jax.random.fold_in(seeds[3], 1), 0, SG - 1).astype(jnp.int32)
    return {"data": data, "templates": templates, "cover": cover, "channel": channel}


EPSILON = 1e-05

def lag_block(length):
    return length // 2 if length >= 256 else length

def toeplitz_rows(weights, block):
    count, length = weights.shape
    period = length + block + 1
    padded = jnp.concatenate([weights, jnp.zeros((count, block + 1), weights.dtype)], axis=1)
    return jnp.tile(padded, (1, block))[:, :block * (length + block)].reshape(count, block, length + block)

def window_blocks(series, length, block):
    count, time_len = series.shape
    ratio = length // block
    split_rows = series.reshape(count, time_len // block, block)
    total = time_len // block - ratio
    parts_list = [split_rows[:, offset:offset + total] for offset in range(ratio + 1)]
    return jnp.concatenate(parts_list, axis=2)

def paired_blocks(series, length):
    count, time_len = series.shape
    split_rows = series.reshape(count, time_len // length, length)
    return jnp.concatenate([split_rows[:, :-1], split_rows[:, 1:]], axis=2)

def reference(data, templates, cover, channel):
    sensor_ids = (cover * (S // N_SENS) + channel).astype(jnp.int32)
    series = data.T
    squares = series.astype(jnp.float32) ** 2
    upper_idx = jnp.arange(2 * L)[None, :]
    lower_idx = jnp.arange(L)[:, None]
    window_band = ((upper_idx >= lower_idx) & (upper_idx < lower_idx + L)).astype(jnp.float32)
    energy = jnp.einsum('skm,um->sku', paired_blocks(squares, L), window_band, precision=lax.Precision.HIGHEST).reshape(S, LAGS)
    stack_gain = math.sqrt(L / C)
    block = lag_block(L)

    def one_template(operands):
        weights, picked = operands
        windows = window_blocks(series[picked].astype(jnp.float32), L, block)
        weights_wide = weights.astype(jnp.float32)
        correlated = jnp.einsum('rkm,rum->rku', windows, toeplitz_rows(weights_wide, block), precision=lax.Precision.HIGHEST).reshape(C, LAGS)
        tmpl_norm = lax.optimization_barrier(jnp.sum(weights_wide * weights_wide, axis=1))
        power_rows = energy[picked]
        scaled = correlated / (L * jnp.sqrt(power_rows / L + EPSILON) * jnp.sqrt(tmpl_norm / L + EPSILON)[:, None])
        return lax.optimization_barrier(jnp.sum(scaled, axis=0)) * stack_gain
    return lax.map(one_template, (templates, sensor_ids))
```

```python
import math

import jax
import jax.numpy as jnp
from jax import lax
from jax.experimental import pallas as pl
from jax.experimental.pallas import tpu as pltpu
from jax.sharding import PartitionSpec as P

EPSILON = 1e-05
LANES = 128
HALF = 64
ROWS = 16
GROUP = 8


def prepare_tables(main_ref, halo_ref, slab, fa, fb, sem, r_ref, g_ref, block, length):
    total = block + length
    strips = main_ref.shape[1] // LANES
    row_count = total // LANES
    lag_rows = block // LANES
    zero_tile = jnp.zeros((LANES, LANES), jnp.float32)
    zero_half = jnp.zeros((HALF, LANES), jnp.float32)

    def copies(strip, slot):
        cols = pl.ds(pl.multiple_of(strip * LANES, LANES), LANES)
        return (
            pltpu.make_async_copy(main_ref.at[:, cols], slab.at[slot, pl.ds(0, block)], sem.at[slot, 0]),
            pltpu.make_async_copy(
                halo_ref.at[:, cols], slab.at[slot, pl.ds(block, length)], sem.at[slot, 1]
            ),
        )

    def windowed(source, target, offsets, count):
        for start in range(0, count, HALF):
            value = source[start : start + HALF, :]
            for offset in offsets:
                value = value + source[start + offset : start + offset + HALF, :]
            target[start : start + HALF, :] = value

    for copy in copies(0, 0):
        copy.start()

    def step(strip, carry):
        slot = lax.rem(strip, 2)

        @pl.when(strip + 1 < strips)
        def _():
            for copy in copies(strip + 1, 1 - slot):
                copy.start()

        for copy in copies(strip, slot):
            copy.wait()
        base = pl.multiple_of(strip * LANES * ROWS, LANES * ROWS)

        def rows(index):
            return pl.ds(base + index, LANES, stride=ROWS)

        for q in range(row_count):
            tile = slab[slot, LANES * q : LANES * (q + 1), :].astype(jnp.float32)
            fa[LANES * q : LANES * (q + 1), :] = tile * tile * 0.5
            r_ref[rows(q), :] = tile.T
        for q in range(row_count, ROWS):
            r_ref[rows(q), :] = zero_tile
        windowed(fa, fb, (1, 2, 3), total)
        windowed(fb, fa, (4,), total)
        windowed(fa, fb, (8, 16, 24), total)
        windowed(fb, fa, (32, 64, 96), total - LANES)
        for start in range(0, block, LANES):
            energy_half = fa[start : start + LANES, :] + fa[start + LANES : start + 2 * LANES, :]
            fb[start : start + LANES, :] = lax.rsqrt(energy_half * (2.0 / length) + EPSILON)

        def half_block(index):
            if 0 <= index < 2 * lag_rows:
                return fb[HALF * index : HALF * (index + 1), :]
            return zero_half

        for parity in range(2):
            for q in range(lag_rows + 1 - parity):
                pair = (half_block(2 * q + parity), half_block(2 * q + parity - 1))
                g_ref[parity, rows(1 + q), :] = jnp.concatenate(pair, axis=0).T
        return carry

    lax.fori_loop(0, strips, step, 0)


def stack_templates(sensor, scale, x_ref, r_ref, g_ref, o_ref, sc, chan_count, lag_rows):
    shift = lax.broadcasted_iota(jnp.int32, (HALF, LANES), 0) + 1
    lane = lax.broadcasted_iota(jnp.int32, (HALF, LANES), 1)
    upper = (lane < HALF) & (lane >= shift)
    zero = jnp.zeros((HALF, LANES), jnp.float32)
    zero_narrow = jnp.zeros((HALF, LANES), jnp.bfloat16)
    low = lax.broadcasted_iota(jnp.int32, (ROWS, LANES), 1) < HALF
    low_out = lax.broadcasted_iota(jnp.int32, (lag_rows, LANES), 1) < HALF

    def one(k, carry):
        first = [jnp.zeros((ROWS, LANES), jnp.float32) for _ in range(2)]
        second = [jnp.zeros((ROWS, LANES), jnp.float32) for _ in range(2)]
        for c in range(chan_count):
            item = k * chan_count + c
            factor = scale[item]
            base = pl.multiple_of(sensor[item] * ROWS, ROWS)
            here = r_ref[pl.ds(base, ROWS), :]
            later = r_ref[pl.ds(base + 2, ROWS), :]
            even = jnp.where(low, here, pltpu.roll(later, HALF, 1))
            odd = jnp.where(low, pltpu.roll(here, HALF, 1), later)
            windows = jnp.concatenate([even, odd], axis=0).astype(jnp.bfloat16)
            lead = jnp.broadcast_to(x_ref[k, 2 * c : 2 * c + 1, :], (HALF, LANES))
            tail = jnp.broadcast_to(x_ref[k, 2 * c + 1 : 2 * c + 2, :], (HALF, LANES))
            lead = pltpu.roll(lead, 1, 1, stride=1, stride_axis=0)
            tail = pltpu.roll(tail, 1, 1, stride=1, stride_axis=0)
            t01 = jnp.where(upper, zero, lead).astype(jnp.bfloat16)
            t23 = jnp.where(upper, lead, tail).astype(jnp.bfloat16)
            t4 = jnp.where(upper, tail, zero).astype(jnp.bfloat16)
            taps = jnp.concatenate(
                [
                    jnp.concatenate([t01, t23], axis=1),
                    jnp.concatenate([t4, zero_narrow], axis=1),
                ],
                axis=0,
            )
            corr = lax.dot_general(
                windows, taps, (((1,), (0,)), ((), ())), preferred_element_type=jnp.float32
            )
            for p in range(2):
                part = corr[ROWS * p : ROWS * (p + 1)]
                first[p] = first[p] + part[:, :LANES] * g_ref[p, pl.ds(base + 1, ROWS), :] * factor
                second[p] = second[p] + part[:, LANES:] * g_ref[p, pl.ds(base, ROWS), :] * factor
        for p in range(2):
            sc[p, 0] = first[p]
            sc[p, 1] = second[p]
        w0 = sc[0, 0, 0:lag_rows] + sc[0, 1, 1 : 1 + lag_rows]
        w0_next = sc[0, 0, 1 : 1 + lag_rows] + sc[0, 1, 2 : 2 + lag_rows]
        w1 = sc[1, 0, 0:lag_rows] + sc[1, 1, 1 : 1 + lag_rows]
        o_ref[pl.ds(k * lag_rows, lag_rows), :] = jnp.where(low_out, w0, w0_next) + pltpu.roll(
            w1, HALF, 1
        )
        return carry

    lax.fori_loop(0, o_ref.shape[0] // lag_rows, one, 0, unroll=4)


def matched_stacks(sensor, scale, taps, main, halo):
    block, sensor_count = main.shape
    length = halo.shape[0]
    count, double, _ = taps.shape
    lag_rows = block // LANES
    total = block + length

    def kernel(sensor, scale, x_ref, main_ref, halo_ref, o_ref, r_ref, g_ref, slab, fa, fb, sc, sem):
        prepare_tables(main_ref, halo_ref, slab, fa, fb, sem, r_ref, g_ref, block, length)
        stack_templates(sensor, scale, x_ref, r_ref, g_ref, o_ref, sc, double // 2, lag_rows)

    single = pl.Buffered(1)
    return pl.pallas_call(
        kernel,
        grid_spec=pltpu.PrefetchScalarGridSpec(
            num_scalar_prefetch=2,
            grid=(1,),
            in_specs=[
                pl.BlockSpec(taps.shape, lambda i, *_: (0, 0, 0), pipeline_mode=single),
                pl.BlockSpec(memory_space=pl.ANY),
                pl.BlockSpec(memory_space=pl.ANY),
            ],
            out_specs=pl.BlockSpec((count * lag_rows, LANES), lambda i, *_: (0, 0), pipeline_mode=single),
            scratch_shapes=[
                pltpu.VMEM((sensor_count * ROWS + 8, LANES), jnp.float32),
                pltpu.VMEM((2, sensor_count * ROWS + 8, LANES), jnp.float32),
                pltpu.VMEM((2, total, LANES), jnp.bfloat16),
                pltpu.VMEM((total + LANES, LANES), jnp.float32),
                pltpu.VMEM((total + LANES, LANES), jnp.float32),
                pltpu.VMEM((2, 2, ROWS, LANES), jnp.float32),
                pltpu.SemaphoreType.DMA((2, 2)),
            ],
        ),
        out_shape=jax.ShapeDtypeStruct((count * lag_rows, LANES), jnp.float32),
        compiler_params=pltpu.CompilerParams(vmem_limit_bytes=62 * 2**20),
    )(sensor, scale, taps, main, halo)


def body(data, templates, cover, channel):
    devices = lax.axis_size("sens")
    layers = devices // GROUP
    per_dev, chan_count, length = templates.shape
    share, sensor_count = data.shape
    sensors_per_group = sensor_count // devices
    block = share * GROUP
    lag_rows = block // LANES
    lag_count = share * devices - length
    in_layer = [[layer * GROUP + j for j in range(GROUP)] for layer in range(layers)]
    across = [[layer * GROUP + j for layer in range(layers)] for j in range(GROUP)]

    main = lax.all_gather(data, "sens", axis_index_groups=in_layer, tiled=True)
    halo = lax.ppermute(
        main[:length], "sens", [(i + GROUP, i) for i in range(devices - GROUP)]
    )
    sensor_own = cover * sensors_per_group + channel
    sensor = lax.all_gather(sensor_own, "sens", axis_index_groups=across, tiled=True)
    weights = lax.all_gather(templates, "sens", axis_index_groups=across, tiled=True)
    count = weights.shape[0]
    wide = weights.astype(jnp.float32)
    power = jnp.sum(wide * wide, axis=2)
    scale = (math.sqrt(length / chan_count) / length) * lax.rsqrt(power / length + EPSILON)
    taps = wide.reshape(count, 2 * chan_count, LANES)[:, :, ::-1]
    stacks = matched_stacks(sensor.reshape(-1), scale.reshape(-1), taps, main, halo)
    spread = lax.all_to_all(
        stacks, "sens", split_axis=0, concat_axis=0, axis_index_groups=across, tiled=True
    )
    spread = spread.reshape(layers, per_dev, lag_rows * LANES)
    return spread.transpose(1, 0, 2).reshape(per_dev, layers * block)[:, :lag_count]


def solution(mesh):
    placed = (P(("parts", "sens"), None), P("sens", None, None), P("sens", None), P("sens", None))
    return jax.shard_map(
        body, mesh=mesh, in_specs=placed, out_specs=P(("parts", "sens"), None), check_vma=False
    )
```

```python
import math

import jax
import jax.numpy as jnp
from jax import lax
from jax.experimental import pallas as pl
from jax.experimental.pallas import tpu as pltpu
from jax.sharding import PartitionSpec as P

EPSILON = 1e-05
LANES = 128
HALF = 64
ROWS = 16
GROUP = 8


def prepare_tables(place, pieces, slab, fa, fb, sem, r_ref, g_ref, block, length):
    total = block + length
    strips = pieces[0].shape[1] // LANES
    row_count = total // LANES
    lag_rows = block // LANES
    zero_tile = jnp.zeros((LANES, LANES), jnp.float32)
    zero_half = jnp.zeros((HALF, LANES), jnp.float32)

    def copies(strip, slot):
        cols = pl.ds(pl.multiple_of(strip * LANES, LANES), LANES)
        made = []
        for i, piece in enumerate(pieces):
            rows = pl.ds(pl.multiple_of(place[i], 16), piece.shape[0])
            made.append(
                pltpu.make_async_copy(piece.at[:, cols], slab.at[slot, rows], sem.at[slot, i])
            )
        return made

    def windowed(source, target, offsets, count):
        for start in range(0, count, HALF):
            value = source[start : start + HALF, :]
            for offset in offsets:
                value = value + source[start + offset : start + offset + HALF, :]
            target[start : start + HALF, :] = value

    for copy in copies(0, 0):
        copy.start()

    def step(strip, carry):
        slot = lax.rem(strip, 2)

        @pl.when(strip + 1 < strips)
        def _():
            for copy in copies(strip + 1, 1 - slot):
                copy.start()

        for copy in copies(strip, slot):
            copy.wait()
        base = pl.multiple_of(strip * LANES * ROWS, LANES * ROWS)

        def rows(index):
            return pl.ds(base + index, LANES, stride=ROWS)

        for q in range(row_count):
            tile = slab[slot, LANES * q : LANES * (q + 1), :].astype(jnp.float32)
            fa[LANES * q : LANES * (q + 1), :] = tile * tile * 0.5
            r_ref[rows(q), :] = tile.T
        for q in range(row_count, ROWS):
            r_ref[rows(q), :] = zero_tile
        windowed(fa, fb, (1, 2, 3), total)
        windowed(fb, fa, (4,), total)
        windowed(fa, fb, (8, 16, 24), total)
        windowed(fb, fa, (32, 64, 96), total - LANES)
        for start in range(0, block, LANES):
            energy_half = fa[start : start + LANES, :] + fa[start + LANES : start + 2 * LANES, :]
            fb[start : start + LANES, :] = lax.rsqrt(energy_half * (2.0 / length) + EPSILON)

        def half_block(index):
            if 0 <= index < 2 * lag_rows:
                return fb[HALF * index : HALF * (index + 1), :]
            return zero_half

        for parity in range(2):
            for q in range(lag_rows + 1 - parity):
                pair = (half_block(2 * q + parity), half_block(2 * q + parity - 1))
                g_ref[parity, rows(1 + q), :] = jnp.concatenate(pair, axis=0).T
        return carry

    lax.fori_loop(0, strips, step, 0)


def stack_templates(sensor, scale, x_ref, r_ref, g_ref, o_ref, sc, chan_count, lag_rows):
    shift = lax.broadcasted_iota(jnp.int32, (HALF, LANES), 0) + 1
    lane = lax.broadcasted_iota(jnp.int32, (HALF, LANES), 1)
    upper = (lane < HALF) & (lane >= shift)
    zero = jnp.zeros((HALF, LANES), jnp.float32)
    zero_narrow = jnp.zeros((HALF, LANES), jnp.bfloat16)
    low = lax.broadcasted_iota(jnp.int32, (ROWS, LANES), 1) < HALF
    low_out = lax.broadcasted_iota(jnp.int32, (lag_rows, LANES), 1) < HALF

    def one(k, carry):
        first = [jnp.zeros((ROWS, LANES), jnp.float32) for _ in range(2)]
        second = [jnp.zeros((ROWS, LANES), jnp.float32) for _ in range(2)]
        for c in range(chan_count):
            item = k * chan_count + c
            factor = scale[item]
            base = pl.multiple_of(sensor[item] * ROWS, ROWS)
            here = r_ref[pl.ds(base, ROWS), :]
            later = r_ref[pl.ds(base + 2, ROWS), :]
            even = jnp.where(low, here, pltpu.roll(later, HALF, 1))
            odd = jnp.where(low, pltpu.roll(here, HALF, 1), later)
            windows = jnp.concatenate([even, odd], axis=0).astype(jnp.bfloat16)
            lead = jnp.broadcast_to(x_ref[k, 2 * c : 2 * c + 1, :], (HALF, LANES))
            tail = jnp.broadcast_to(x_ref[k, 2 * c + 1 : 2 * c + 2, :], (HALF, LANES))
            lead = pltpu.roll(lead, 1, 1, stride=1, stride_axis=0)
            tail = pltpu.roll(tail, 1, 1, stride=1, stride_axis=0)
            t01 = jnp.where(upper, zero, lead).astype(jnp.bfloat16)
            t23 = jnp.where(upper, lead, tail).astype(jnp.bfloat16)
            t4 = jnp.where(upper, tail, zero).astype(jnp.bfloat16)
            taps = jnp.concatenate(
                [
                    jnp.concatenate([t01, t23], axis=1),
                    jnp.concatenate([t4, zero_narrow], axis=1),
                ],
                axis=0,
            )
            corr = lax.dot_general(
                windows, taps, (((1,), (0,)), ((), ())), preferred_element_type=jnp.float32
            )
            for p in range(2):
                part = corr[ROWS * p : ROWS * (p + 1)]
                first[p] = first[p] + part[:, :LANES] * g_ref[p, pl.ds(base + 1, ROWS), :] * factor
                second[p] = second[p] + part[:, LANES:] * g_ref[p, pl.ds(base, ROWS), :] * factor
        for p in range(2):
            sc[p, 0] = first[p]
            sc[p, 1] = second[p]
        w0 = sc[0, 0, 0:lag_rows] + sc[0, 1, 1 : 1 + lag_rows]
        w0_next = sc[0, 0, 1 : 1 + lag_rows] + sc[0, 1, 2 : 2 + lag_rows]
        w1 = sc[1, 0, 0:lag_rows] + sc[1, 1, 1 : 1 + lag_rows]
        o_ref[pl.ds(k * lag_rows, lag_rows), :] = jnp.where(low_out, w0, w0_next) + pltpu.roll(
            w1, HALF, 1
        )
        return carry

    lax.fori_loop(0, o_ref.shape[0] // lag_rows, one, 0, unroll=4)


def matched_stacks(sensor, scale, place, taps, pieces, block, length):
    sensor_count = pieces[0].shape[1]
    count, double, _ = taps.shape
    lag_rows = block // LANES
    total = block + length
    held = block + 2 * pieces[0].shape[0]
    piece_count = len(pieces)

    def kernel(sensor, scale, place, x_ref, *refs):
        ins = refs[:piece_count]
        o_ref, r_ref, g_ref, slab, fa, fb, sc, sem = refs[piece_count:]
        prepare_tables(place, ins, slab, fa, fb, sem, r_ref, g_ref, block, length)
        stack_templates(sensor, scale, x_ref, r_ref, g_ref, o_ref, sc, double // 2, lag_rows)

    single = pl.Buffered(1)
    return pl.pallas_call(
        kernel,
        grid_spec=pltpu.PrefetchScalarGridSpec(
            num_scalar_prefetch=3,
            grid=(1,),
            in_specs=[pl.BlockSpec(taps.shape, lambda i, *_: (0, 0, 0), pipeline_mode=single)]
            + [pl.BlockSpec(memory_space=pl.ANY)] * piece_count,
            out_specs=pl.BlockSpec((count * lag_rows, LANES), lambda i, *_: (0, 0), pipeline_mode=single),
            scratch_shapes=[
                pltpu.VMEM((sensor_count * ROWS + 8, LANES), jnp.float32),
                pltpu.VMEM((2, sensor_count * ROWS + 8, LANES), jnp.float32),
                pltpu.VMEM((2, held, LANES), jnp.bfloat16),
                pltpu.VMEM((total + LANES, LANES), jnp.float32),
                pltpu.VMEM((total + LANES, LANES), jnp.float32),
                pltpu.VMEM((2, 2, ROWS, LANES), jnp.float32),
                pltpu.SemaphoreType.DMA((2, piece_count)),
            ],
        ),
        out_shape=jax.ShapeDtypeStruct((count * lag_rows, LANES), jnp.float32),
        compiler_params=pltpu.CompilerParams(vmem_limit_bytes=62 * 2**20),
    )(sensor, scale, place, taps, *pieces)


def body(data, templates, cover, channel):
    devices = lax.axis_size("sens")
    layers = devices // GROUP
    per_dev, chan_count, length = templates.shape
    share, sensor_count = data.shape
    sensors_per_group = sensor_count // devices
    block = share * GROUP
    lag_rows = block // LANES
    lag_count = share * devices - length
    half = share // 2
    me = lax.axis_index("sens")
    layer, inner = me // GROUP, me % GROUP

    def flip(value, bits):
        return lax.ppermute(value, "sens", [(i, i ^ bits) for i in range(devices)])

    item_rows = per_dev * 2 * chan_count
    id_rows = per_dev * chan_count // LANES
    reversed_halves = templates.reshape(item_rows, LANES)[:, ::-1]
    pad_rows = -(item_rows + 2 * id_rows) % 16
    packet = jnp.concatenate(
        [
            reversed_halves,
            cover.reshape(id_rows, LANES).astype(jnp.bfloat16),
            channel.reshape(id_rows, LANES).astype(jnp.bfloat16),
            jnp.zeros((pad_rows, LANES), jnp.bfloat16),
        ],
        axis=0,
    )

    near = flip(data, 2)
    side = flip(data, 4)
    packets = [flip(packet, GROUP * q) for q in reversed(range(1, layers))]
    twin = flip(data, 1)
    far_low = flip(near[:half], 4)
    far_high = flip(side[half:], 2)
    near_twin = flip(near, 1)
    side_twin = flip(side, 1)
    far_low_twin = flip(far_low, 1)
    far_high_twin = flip(far_high, 1)
    far = jnp.concatenate([far_low, far_high], axis=0)
    chip = inner // 2
    lead = jnp.where(
        chip == 0, data, jnp.where(chip == 1, near, jnp.where(chip == 2, side, far))
    )
    held = lax.optimization_barrier(
        (lead, *packets, twin, near_twin, side_twin, far_low_twin, far_high_twin)
    )
    lead, packets = held[0], [packet] + list(held[1:layers][::-1])
    twin, near_twin, side_twin, far_low_twin, far_high_twin = held[layers:]
    halo = lax.ppermute(lead, "sens", [(i + GROUP, i) for i in range(devices - GROUP)])
    halo_twin = flip(halo, 1)
    pieces = [
        data, near, side, twin, near_twin, side_twin,
        far_low, far_high, far_low_twin, far_high_twin, halo, halo_twin,
    ]
    core = inner % 2
    starts = [share * (inner ^ r) for r in (0, 2, 4, 1, 3, 5)]
    starts += [share * (inner ^ 6), share * (inner ^ 6) + half]
    starts += [share * (inner ^ 7), share * (inner ^ 7) + half]
    starts += [block + share * core, block + share * (1 - core)]
    place = jnp.stack(starts).astype(jnp.int32)

    gathered = jnp.stack(packets)
    count = layers * per_dev
    wide = gathered[:, :item_rows].astype(jnp.float32).reshape(count, 2 * chan_count, LANES)
    ids = gathered[:, item_rows : item_rows + 2 * id_rows].astype(jnp.int32)
    sensor = (ids[:, :id_rows] * sensors_per_group + ids[:, id_rows:]).reshape(-1)
    power = jnp.sum((wide * wide).reshape(count, chan_count, length), axis=2)
    scale = (math.sqrt(length / chan_count) / length) * lax.rsqrt(power / length + EPSILON)

    stacks = matched_stacks(sensor, scale.reshape(-1), place, wide, pieces, block, length)
    parts = stacks.reshape(layers, per_dev * lag_rows, LANES)
    received = [parts[0]] + [flip(parts[q], GROUP * q) for q in range(1, layers)]
    ordered = []
    for slot in range(layers):
        value = received[slot]
        for mine in range(1, layers):
            value = jnp.where(layer == mine, received[slot ^ mine], value)
        ordered.append(value.reshape(per_dev, block))
    return jnp.concatenate(ordered, axis=1)[:, :lag_count]


def solution(mesh):
    placed = (P(("parts", "sens"), None), P("sens", None, None), P("sens", None), P("sens", None))
    return jax.shard_map(
        body, mesh=mesh, in_specs=placed, out_specs=P(("parts", "sens"), None), check_vma=False
    )
```

```python
import math

import jax
import jax.numpy as jnp
from jax import lax
from jax.experimental import pallas as pl
from jax.experimental.pallas import tpu as pltpu
from jax.sharding import PartitionSpec as P

EPSILON = 1e-05
LANES = 128
HALF = 64
ROWS = 16
GROUP = 8
SLOTS = 4
STAGE_ROWS = 33


def prepare_tables(place, pieces, slab, stage, fa, fb, sem, w_ref, g_ref, block, length):
    total = block + length
    strips = pieces[0].shape[1] // LANES
    lag_rows = block // LANES
    norm_rows = lag_rows + 3
    double = 2 * ROWS
    zero_half = jnp.zeros((HALF, LANES), jnp.float32)

    def copies(strip, slot):
        cols = pl.ds(pl.multiple_of(strip * LANES, LANES), LANES)
        made = []
        for i, piece in enumerate(pieces):
            rows = pl.ds(pl.multiple_of(place[i], 16), piece.shape[0])
            made.append(
                pltpu.make_async_copy(piece.at[:, cols], slab.at[slot, rows], sem.at[slot, i])
            )
        return made

    def windowed(source, target, offsets, count):
        for start in range(0, count, HALF):
            value = source[start : start + HALF, :]
            for offset in offsets:
                value = value + source[start + offset : start + offset + HALF, :]
            target[start : start + HALF, :] = value

    for ahead in range(SLOTS - 1):
        for copy in copies(ahead, ahead):
            copy.start()
    for start in range(0, LANES * STAGE_ROWS, LANES):
        stage[start : start + LANES, :] = jnp.zeros((LANES, LANES), jnp.float32)

    def step(strip, carry):
        slot = lax.rem(strip, SLOTS)

        @pl.when(strip + SLOTS - 1 < strips)
        def _():
            for copy in copies(strip + SLOTS - 1, lax.rem(strip + SLOTS - 1, SLOTS)):
                copy.start()

        for copy in copies(strip, slot):
            copy.wait()

        def samples(index):
            if HALF * (index + 1) <= total:
                return slab[slot, HALF * index : HALF * (index + 1), :].astype(jnp.float32)
            return zero_half

        for index in range(total // HALF):
            value = samples(index)
            fa[HALF * index : HALF * (index + 1), :] = value * value * 0.5
        for parity in range(2):
            for q in range(total // LANES):
                index = 2 * q + parity
                tile = jnp.concatenate([samples(index), samples(index + length // HALF)], axis=0)
                stage[pl.ds(ROWS * parity + q, LANES, stride=STAGE_ROWS), :] = tile.T
        base = pl.multiple_of(strip * LANES * double, LANES * double)
        for item in range(LANES):
            rows = stage[STAGE_ROWS * item : STAGE_ROWS * item + double, :]
            w_ref[pl.ds(base + double * item, double), :] = rows.astype(jnp.bfloat16)
        windowed(fa, fb, (1, 2, 3), total)
        windowed(fb, fa, (4,), total)
        windowed(fa, fb, (8, 16, 24), total)
        windowed(fb, fa, (32, 64, 96), total - LANES)
        for start in range(0, block, LANES):
            energy_half = fa[start : start + LANES, :] + fa[start + LANES : start + 2 * LANES, :]
            fb[start : start + LANES, :] = lax.rsqrt(energy_half * (2.0 / length) + EPSILON)

        def half_block(index):
            if 0 <= index < 2 * lag_rows:
                return fb[HALF * index : HALF * (index + 1), :]
            return zero_half

        base = strip * (LANES * norm_rows)
        for parity in range(2):
            for q in range(lag_rows + 1 - parity):
                pair = (half_block(2 * q + parity), half_block(2 * q + parity - 1))
                rows = pl.ds(base + 1 + q, LANES, stride=norm_rows)
                g_ref[parity, rows, :] = jnp.concatenate(pair, axis=0).T
        return carry

    lax.fori_loop(0, strips, step, 0)


def stack_templates(sensor, scale, x_ref, w_ref, g_ref, o_ref, sc, first_k, count, chan_count, lag_rows):
    shift = lax.broadcasted_iota(jnp.int32, (HALF, LANES), 0) + 1
    lane = lax.broadcasted_iota(jnp.int32, (HALF, LANES), 1)
    upper = (lane < HALF) & (lane >= shift)
    zero = jnp.zeros((HALF, LANES), jnp.float32)
    zero_narrow = jnp.zeros((HALF, LANES), jnp.bfloat16)
    low_out = lax.broadcasted_iota(jnp.int32, (lag_rows, LANES), 1) < HALF

    def one(step, carry):
        k = first_k + step
        first = [jnp.zeros((ROWS, LANES), jnp.float32) for _ in range(2)]
        second = [jnp.zeros((ROWS, LANES), jnp.float32) for _ in range(2)]
        for c in range(chan_count):
            item = k * chan_count + c
            factor = scale[item]
            base = sensor[item] * (lag_rows + 3)
            windows = w_ref[pl.ds(pl.multiple_of(sensor[item] * 2 * ROWS, 2 * ROWS), 2 * ROWS), :]
            lead = jnp.broadcast_to(x_ref[k, 2 * c : 2 * c + 1, :], (HALF, LANES))
            tail = jnp.broadcast_to(x_ref[k, 2 * c + 1 : 2 * c + 2, :], (HALF, LANES))
            lead = pltpu.roll(lead, 1, 1, stride=1, stride_axis=0)
            tail = pltpu.roll(tail, 1, 1, stride=1, stride_axis=0)
            t01 = jnp.where(upper, zero, lead).astype(jnp.bfloat16)
            t23 = jnp.where(upper, lead, tail).astype(jnp.bfloat16)
            t4 = jnp.where(upper, tail, zero).astype(jnp.bfloat16)
            taps = jnp.concatenate(
                [
                    jnp.concatenate([t01, t23], axis=1),
                    jnp.concatenate([t4, zero_narrow], axis=1),
                ],
                axis=0,
            )
            corr = lax.dot_general(
                windows, taps, (((1,), (0,)), ((), ())), preferred_element_type=jnp.float32
            )
            for p in range(2):
                part = corr[ROWS * p : ROWS * (p + 1)]
                first[p] = first[p] + part[:, :LANES] * g_ref[p, pl.ds(base + 1, ROWS), :] * factor
                second[p] = second[p] + part[:, LANES:] * g_ref[p, pl.ds(base, ROWS), :] * factor
        for p in range(2):
            sc[p, 0] = first[p]
            sc[p, 1] = second[p]
        w0 = sc[0, 0, 0:lag_rows] + sc[0, 1, 1 : 1 + lag_rows]
        w0_next = sc[0, 0, 1 : 1 + lag_rows] + sc[0, 1, 2 : 2 + lag_rows]
        w1 = sc[1, 0, 0:lag_rows] + sc[1, 1, 1 : 1 + lag_rows]
        o_ref[pl.ds(k * lag_rows, lag_rows), :] = jnp.where(low_out, w0, w0_next) + pltpu.roll(
            w1, HALF, 1
        )
        return carry

    lax.fori_loop(0, count, one, 0, unroll=4)


def matched_stacks(sensor, scale, place, taps, pieces, block, length, layers):
    sensor_count = pieces[0].shape[1]
    count, double, _ = taps.shape
    lag_rows = block // LANES
    total = block + length
    held = block + 2 * pieces[0].shape[0]
    piece_count = len(pieces)
    part = count // layers

    def kernel(sensor, scale, place, x_hbm, *refs):
        ins = refs[:piece_count]
        out, x_ref, o_ref, w_ref, g_ref, slab, stage, fa, fb, sc, sem, side_sem = refs[piece_count:]
        load = pltpu.make_async_copy(x_hbm, x_ref, side_sem.at[layers])
        load.start()
        prepare_tables(place, ins, slab, stage, fa, fb, sem, w_ref, g_ref, block, length)
        load.wait()

        def stores(q):
            rows = pl.ds(pl.multiple_of(q * part * lag_rows, 8), part * lag_rows)
            return pltpu.make_async_copy(o_ref.at[rows], out.at[rows], side_sem.at[q])

        def chunk(q, carry):
            stack_templates(
                sensor, scale, x_ref, w_ref, g_ref, o_ref, sc, q * part, part, double // 2, lag_rows
            )
            stores(q).start()
            return carry

        lax.fori_loop(0, layers, chunk, 0)
        for q in range(layers):
            stores(q).wait()

    return pl.pallas_call(
        kernel,
        grid_spec=pltpu.PrefetchScalarGridSpec(
            num_scalar_prefetch=3,
            grid=(1,),
            in_specs=[pl.BlockSpec(memory_space=pl.ANY)] * (1 + piece_count),
            out_specs=pl.BlockSpec(memory_space=pl.ANY),
            scratch_shapes=[
                pltpu.VMEM(taps.shape, jnp.float32),
                pltpu.VMEM((count * lag_rows, LANES), jnp.float32),
                pltpu.VMEM((sensor_count * 2 * ROWS, LANES), jnp.bfloat16),
                pltpu.VMEM((2, sensor_count * (lag_rows + 3) + 8, LANES), jnp.float32),
                pltpu.VMEM((SLOTS, held, LANES), jnp.bfloat16),
                pltpu.VMEM((STAGE_ROWS * LANES, LANES), jnp.float32),
                pltpu.VMEM((total + LANES, LANES), jnp.float32),
                pltpu.VMEM((total + LANES, LANES), jnp.float32),
                pltpu.VMEM((2, 2, ROWS, LANES), jnp.float32),
                pltpu.SemaphoreType.DMA((SLOTS, piece_count)),
                pltpu.SemaphoreType.DMA((layers + 1,)),
            ],
        ),
        out_shape=jax.ShapeDtypeStruct((count * lag_rows, LANES), jnp.float32),
        compiler_params=pltpu.CompilerParams(vmem_limit_bytes=62 * 2**20),
    )(sensor, scale, place, taps, *pieces)


def body(data, templates, cover, channel):
    devices = lax.axis_size("sens")
    layers = devices // GROUP
    per_dev, chan_count, length = templates.shape
    share, sensor_count = data.shape
    sensors_per_group = sensor_count // devices
    block = share * GROUP
    lag_rows = block // LANES
    lag_count = share * devices - length
    half = share // 2
    me = lax.axis_index("sens")
    layer, inner = me // GROUP, me % GROUP

    def flip(value, bits):
        return lax.ppermute(value, "sens", [(i, i ^ bits) for i in range(devices)])

    item_rows = per_dev * 2 * chan_count
    id_rows = per_dev * chan_count // LANES
    reversed_halves = templates.reshape(item_rows, LANES)[:, ::-1]
    pad_rows = -(item_rows + 2 * id_rows) % 16
    packet = jnp.concatenate(
        [
            reversed_halves,
            cover.reshape(id_rows, LANES).astype(jnp.bfloat16),
            channel.reshape(id_rows, LANES).astype(jnp.bfloat16),
            jnp.zeros((pad_rows, LANES), jnp.bfloat16),
        ],
        axis=0,
    )

    near = flip(data, 2)
    side = flip(data, 4)
    packets = [flip(packet, GROUP * q) for q in reversed(range(1, layers))]
    twin = flip(data, 1)
    far_low = flip(near[:half], 4)
    far_high = flip(side[half:], 2)
    near_twin = flip(near, 1)
    side_twin = flip(side, 1)
    far_low_twin = flip(far_low, 1)
    far_high_twin = flip(far_high, 1)
    far = jnp.concatenate([far_low, far_high], axis=0)
    chip = inner // 2
    lead = jnp.where(
        chip == 0, data, jnp.where(chip == 1, near, jnp.where(chip == 2, side, far))
    )
    held = lax.optimization_barrier(
        (lead, *packets, twin, near_twin, side_twin, far_low_twin, far_high_twin)
    )
    lead, packets = held[0], [packet] + list(held[1:layers][::-1])
    twin, near_twin, side_twin, far_low_twin, far_high_twin = held[layers:]
    halo = lax.ppermute(lead, "sens", [(i + GROUP, i) for i in range(devices - GROUP)])
    halo_twin = flip(halo, 1)
    pieces = [
        data, near, side, twin, near_twin, side_twin,
        far_low, far_high, far_low_twin, far_high_twin, halo, halo_twin,
    ]
    core = inner % 2
    starts = [share * (inner ^ r) for r in (0, 2, 4, 1, 3, 5)]
    starts += [share * (inner ^ 6), share * (inner ^ 6) + half]
    starts += [share * (inner ^ 7), share * (inner ^ 7) + half]
    starts += [block + share * core, block + share * (1 - core)]
    place = jnp.stack(starts).astype(jnp.int32)

    gathered = jnp.stack(packets)
    count = layers * per_dev
    wide = gathered[:, :item_rows].astype(jnp.float32).reshape(count, 2 * chan_count, LANES)
    ids = gathered[:, item_rows : item_rows + 2 * id_rows].astype(jnp.int32)
    sensor = (ids[:, :id_rows] * sensors_per_group + ids[:, id_rows:]).reshape(-1)
    power = jnp.sum((wide * wide).reshape(count, chan_count, length), axis=2)
    scale = (math.sqrt(length / chan_count) / length) * lax.rsqrt(power / length + EPSILON)

    stacks = matched_stacks(sensor, scale.reshape(-1), place, wide, pieces, block, length, layers)
    parts = stacks.reshape(layers, per_dev * lag_rows, LANES)
    received = [parts[0]] + [flip(parts[q], GROUP * q) for q in range(1, layers)]
    ordered = []
    for slot in range(layers):
        value = received[slot]
        for mine in range(1, layers):
            value = jnp.where(layer == mine, received[slot ^ mine], value)
        ordered.append(value.reshape(per_dev, block))
    return jnp.concatenate(ordered, axis=1)[:, :lag_count]


def solution(mesh):
    placed = (P(("parts", "sens"), None), P("sens", None, None), P("sens", None), P("sens", None))
    return jax.shard_map(
        body, mesh=mesh, in_specs=placed, out_specs=P(("parts", "sens"), None), check_vma=False
    )
```

```python
import math

import jax
import jax.numpy as jnp
from jax import lax
from jax.experimental import pallas as pl
from jax.experimental.pallas import tpu as pltpu
from jax.sharding import PartitionSpec as P

EPSILON = 1e-05
LANES = 128
HALF = 64
ROWS = 16
GROUP = 8
SLOTS = 4
VMEM_LIMIT = 14 * 2**20
STAGE_ROWS = 33


def start_strip_copies(place, pieces, slab, sem, strip, slot):
    cols = pl.ds(pl.multiple_of(strip * LANES, LANES), LANES)
    made = []
    for i, piece in enumerate(pieces):
        rows = pl.ds(pl.multiple_of(place[i], 16), piece.shape[0])
        made.append(pltpu.make_async_copy(piece.at[:, cols], slab.at[slot, rows], sem.at[slot, i]))
    return made


def for_each_strip(place, pieces, slab, sem, work):
    strips = pieces[0].shape[1] // LANES
    for ahead in range(SLOTS - 1):
        for copy in start_strip_copies(place, pieces, slab, sem, ahead, ahead):
            copy.start()

    def step(strip, carry):
        slot = lax.rem(strip, SLOTS)
        coming = strip + SLOTS - 1

        @pl.when(coming < strips)
        def _():
            for copy in start_strip_copies(place, pieces, slab, sem, coming, lax.rem(coming, SLOTS)):
                copy.start()

        for copy in start_strip_copies(place, pieces, slab, sem, strip, slot):
            copy.wait()
        work(strip, slot)
        return carry

    lax.fori_loop(0, strips, step, 0)


def windowed(source, target, offsets, count):
    for start in range(0, count, HALF):
        value = source[start : start + HALF, :]
        for offset in offsets:
            value = value + source[start + offset : start + offset + HALF, :]
        target[start : start + HALF, :] = value


def table_part(strip, samples, stage, fa, fb, w_ref, g_ref, span, norms, rows, lag_rows, length):
    double = 2 * ROWS
    norm_rows = lag_rows + 3
    origin, limit = span
    first, last = rows
    for index in range(origin, limit):
        value = samples(index)
        at = HALF * (index - origin)
        fa[at : at + HALF, :] = value * value * 0.5
    for parity in range(2):
        for q in range(first, last):
            index = 2 * q + parity
            tile = jnp.concatenate([samples(index), samples(index + length // HALF)], axis=0)
            stage[pl.ds(ROWS * parity + q, LANES, stride=STAGE_ROWS), :] = tile.T
    base = pl.multiple_of(strip * LANES * double, LANES * double)
    top = min(ROWS, -(-last // 8) * 8)
    for item in range(LANES):
        for parity in range(2):
            low = ROWS * parity
            value = stage[STAGE_ROWS * item + low + first : STAGE_ROWS * item + low + top, :]
            target = pl.ds(base + double * item + low + first, top - first)
            w_ref[target, :] = value.astype(jnp.bfloat16)
    count = HALF * (limit - origin)
    windowed(fa, fb, (1, 2, 3), count)
    windowed(fb, fa, (4,), count)
    windowed(fa, fb, (8, 16, 24), count)
    windowed(fb, fa, (32, 64, 96), count - LANES)
    for index in range(*norms):
        at = HALF * (index - origin)
        energy_half = fa[at : at + HALF, :] + fa[at + LANES : at + LANES + HALF, :]
        fb[at : at + HALF, :] = lax.rsqrt(energy_half * (2.0 / length) + EPSILON)

    def norm_block(index):
        if norms[0] <= index < norms[1]:
            return fb[HALF * (index - origin) : HALF * (index - origin + 1), :]
        return jnp.zeros((HALF, LANES), jnp.float32)

    base = strip * (LANES * norm_rows)
    for parity in range(2):
        for q in range(first, min(last, lag_rows + 1 - parity)):
            pair = (norm_block(2 * q + parity), norm_block(2 * q + parity - 1))
            target = pl.ds(base + 1 + q, LANES, stride=norm_rows)
            g_ref[parity, target, :] = jnp.concatenate(pair, axis=0).T


def clear(stage):
    for start in range(0, LANES * STAGE_ROWS, LANES):
        stage[start : start + LANES, :] = jnp.zeros((LANES, LANES), jnp.float32)


def stack_templates(sensor, scale, x_ref, w_ref, g_ref, o_ref, sc, first, offset, chan_count, lag_rows):
    shift = lax.broadcasted_iota(jnp.int32, (HALF, LANES), 0) + 1
    lane = lax.broadcasted_iota(jnp.int32, (HALF, LANES), 1)
    upper = (lane < HALF) & (lane >= shift)
    zero = jnp.zeros((HALF, LANES), jnp.float32)
    zero_narrow = jnp.zeros((HALF, LANES), jnp.bfloat16)
    low_out = lax.broadcasted_iota(jnp.int32, (lag_rows, LANES), 1) < HALF

    def one(step, carry):
        k = offset + step
        leading = [jnp.zeros((ROWS, LANES), jnp.float32) for _ in range(2)]
        trailing = [jnp.zeros((ROWS, LANES), jnp.float32) for _ in range(2)]
        for c in range(chan_count):
            item = (first + step) * chan_count + c
            factor = scale[item]
            base = sensor[item] * (lag_rows + 3)
            windows = w_ref[pl.ds(pl.multiple_of(sensor[item] * 2 * ROWS, 2 * ROWS), 2 * ROWS), :]
            lead = jnp.broadcast_to(x_ref[k, 2 * c : 2 * c + 1, :], (HALF, LANES))
            tail = jnp.broadcast_to(x_ref[k, 2 * c + 1 : 2 * c + 2, :], (HALF, LANES))
            lead = pltpu.roll(lead, 1, 1, stride=1, stride_axis=0)
            tail = pltpu.roll(tail, 1, 1, stride=1, stride_axis=0)
            t01 = jnp.where(upper, zero, lead).astype(jnp.bfloat16)
            t23 = jnp.where(upper, lead, tail).astype(jnp.bfloat16)
            t4 = jnp.where(upper, tail, zero).astype(jnp.bfloat16)
            taps = jnp.concatenate(
                [
                    jnp.concatenate([t01, t23], axis=1),
                    jnp.concatenate([t4, zero_narrow], axis=1),
                ],
                axis=0,
            )
            corr = lax.dot_general(
                windows, taps, (((1,), (0,)), ((), ())), preferred_element_type=jnp.float32
            )
            for p in range(2):
                part = corr[ROWS * p : ROWS * (p + 1)]
                leading[p] = leading[p] + part[:, :LANES] * g_ref[p, pl.ds(base + 1, ROWS), :] * factor
                trailing[p] = trailing[p] + part[:, LANES:] * g_ref[p, pl.ds(base, ROWS), :] * factor
        for p in range(2):
            sc[p, 0] = leading[p]
            sc[p, 1] = trailing[p]
        w0 = sc[0, 0, 0:lag_rows] + sc[0, 1, 1 : 1 + lag_rows]
        w0_next = sc[0, 0, 1 : 1 + lag_rows] + sc[0, 1, 2 : 2 + lag_rows]
        w1 = sc[1, 0, 0:lag_rows] + sc[1, 1, 1 : 1 + lag_rows]
        o_ref[pl.ds(step * lag_rows, lag_rows), :] = jnp.where(low_out, w0, w0_next) + pltpu.roll(
            w1, HALF, 1
        )
        return carry

    lax.fori_loop(0, o_ref.shape[0] // lag_rows, one, 0, unroll=4)


def in_vmem(value):
    return pltpu.with_memory_space_constraint(value, pltpu.VMEM)


def cost(microseconds):
    return pl.CostEstimate(
        flops=int(microseconds * 1e9), bytes_accessed=int(microseconds * 1e6), transcendentals=0
    )


def early_tables(place, pieces, block, length):
    sensor_count = pieces[0].shape[1]
    strips = sensor_count // LANES
    lag_rows = block // LANES
    local = (block - length) // HALF
    kept = block - HALF * (local - 1)
    piece_count = len(pieces)

    def kernel(place, *refs):
        ins = refs[:piece_count]
        w_ref, g_ref, tail_ref, slab, stage, fa, fb, sem = refs[piece_count:]
        clear(stage)

        def work(strip, slot):
            def samples(index):
                return slab[slot, HALF * index : HALF * (index + 1), :].astype(jnp.float32)

            tail_ref[strip] = slab[slot, block - kept : block, :]
            table_part(
                strip, samples, stage, fa, fb, w_ref, g_ref,
                (0, block // HALF), (0, local), (0, local // 2), lag_rows, length,
            )

        for_each_strip(place, ins, slab, sem, work)

    whole = pl.BlockSpec(memory_space=pltpu.VMEM)
    return pl.pallas_call(
        kernel,
        grid_spec=pltpu.PrefetchScalarGridSpec(
            num_scalar_prefetch=1,
            grid=(),
            in_specs=[pl.BlockSpec(memory_space=pl.ANY)] * piece_count,
            out_specs=(whole, whole, whole),
            scratch_shapes=[
                pltpu.VMEM((SLOTS, block, LANES), jnp.bfloat16),
                pltpu.VMEM((STAGE_ROWS * LANES, LANES), jnp.float32),
                pltpu.VMEM((block + LANES, LANES), jnp.float32),
                pltpu.VMEM((block + LANES, LANES), jnp.float32),
                pltpu.SemaphoreType.DMA((SLOTS, piece_count)),
            ],
        ),
        out_shape=(
            pltpu.VMEM((sensor_count * 2 * ROWS, LANES), jnp.bfloat16),
            pltpu.VMEM((2, sensor_count * (lag_rows + 3) + 8, LANES), jnp.float32),
            pltpu.VMEM((strips, kept, LANES), jnp.bfloat16),
        ),
        compiler_params=pltpu.CompilerParams(vmem_limit_bytes=VMEM_LIMIT),
    )(place, *pieces)


def late_tables(place, pieces, early, block, length):
    lag_rows = block // LANES
    local = (block - length) // HALF
    total = (block + length) // HALF
    inside = block // HALF
    piece_count = len(pieces)

    def kernel(place, tail_ref, w_in, g_in, *refs):
        ins = refs[:piece_count]
        w_ref, g_ref, slab, stage, fa, fb, sem = refs[piece_count:]
        clear(stage)

        def work(strip, slot):
            def samples(index):
                if index < inside:
                    at = HALF * (index - local + 1)
                    return tail_ref[strip, at : at + HALF, :].astype(jnp.float32)
                if index < total:
                    at = HALF * (index - inside)
                    return slab[slot, at : at + HALF, :].astype(jnp.float32)
                return jnp.zeros((HALF, LANES), jnp.float32)

            table_part(
                strip, samples, stage, fa, fb, w_ref, g_ref,
                (local - 1, total), (local - 1, inside), (local // 2, total // 2), lag_rows, length,
            )

        for_each_strip(place, ins, slab, sem, work)

    whole = pl.BlockSpec(memory_space=pltpu.VMEM)
    span = HALF * (total - local + 1)
    return pl.pallas_call(
        kernel,
        grid_spec=pltpu.PrefetchScalarGridSpec(
            num_scalar_prefetch=1,
            grid=(),
            in_specs=[whole, whole, whole] + [pl.BlockSpec(memory_space=pl.ANY)] * piece_count,
            out_specs=(whole, whole),
            scratch_shapes=[
                pltpu.VMEM((SLOTS, 2 * pieces[0].shape[0], LANES), jnp.bfloat16),
                pltpu.VMEM((STAGE_ROWS * LANES, LANES), jnp.float32),
                pltpu.VMEM((span + LANES, LANES), jnp.float32),
                pltpu.VMEM((span + LANES, LANES), jnp.float32),
                pltpu.SemaphoreType.DMA((SLOTS, piece_count)),
            ],
        ),
        out_shape=(
            pltpu.VMEM(early[0].shape, early[0].dtype),
            pltpu.VMEM(early[1].shape, early[1].dtype),
        ),
        input_output_aliases={2: 0, 3: 1},
        compiler_params=pltpu.CompilerParams(vmem_limit_bytes=VMEM_LIMIT),
    )(place, in_vmem(early[2]), in_vmem(early[0]), in_vmem(early[1]), *pieces)


def matched_stacks(sensor, scale, taps, tables, per_dev, lag_rows):
    count, double, _ = taps.shape
    number = count // per_dev

    def kernel(sensor, scale, x_ref, w_ref, g_ref, *refs):
        for i in range(number):
            stack_templates(
                sensor, scale, x_ref, w_ref, g_ref, refs[i], refs[number],
                i * per_dev, i * per_dev, double // 2, lag_rows,
            )

    whole = pl.BlockSpec(memory_space=pltpu.VMEM)
    return pl.pallas_call(
        kernel,
        grid_spec=pltpu.PrefetchScalarGridSpec(
            num_scalar_prefetch=2,
            grid=(),
            in_specs=[whole, whole, whole],
            out_specs=[whole] * number,
            scratch_shapes=[pltpu.VMEM((2, 2, ROWS, LANES), jnp.float32)],
        ),
        out_shape=[jax.ShapeDtypeStruct((per_dev * lag_rows, LANES), jnp.float32)] * number,
        compiler_params=pltpu.CompilerParams(vmem_limit_bytes=VMEM_LIMIT),
        cost_estimate=cost(8 * number),
    )(sensor, scale, taps, in_vmem(tables[0]), in_vmem(tables[1]))


def body(data, templates, cover, channel):
    devices = lax.axis_size("sens")
    layers = devices // GROUP
    per_dev, chan_count, length = templates.shape
    share, sensor_count = data.shape
    sensors_per_group = sensor_count // devices
    block = share * GROUP
    lag_rows = block // LANES
    lag_count = share * devices - length
    half = share // 2
    me = lax.axis_index("sens")
    layer, inner = me // GROUP, me % GROUP

    def flip(value, bits):
        return lax.ppermute(value, "sens", [(i, i ^ bits) for i in range(devices)])

    item_rows = per_dev * 2 * chan_count
    id_rows = per_dev * chan_count // LANES
    reversed_halves = templates.reshape(item_rows, LANES)[:, ::-1]
    pad_rows = -(item_rows + 2 * id_rows) % 16
    packet = jnp.concatenate(
        [
            reversed_halves,
            cover.reshape(id_rows, LANES).astype(jnp.bfloat16),
            channel.reshape(id_rows, LANES).astype(jnp.bfloat16),
            jnp.zeros((pad_rows, LANES), jnp.bfloat16),
        ],
        axis=0,
    )

    near = flip(data, 2)
    side = flip(data, 4)
    packets = [flip(packet, GROUP * q) for q in reversed(range(1, layers))]
    twin = flip(data, 1)
    far_low = flip(near[:half], 4)
    far_high = flip(side[half:], 2)
    near_twin = flip(near, 1)
    side_twin = flip(side, 1)
    far_low_twin = flip(far_low, 1)
    far_high_twin = flip(far_high, 1)
    far = jnp.concatenate([far_low, far_high], axis=0)
    chip = inner // 2
    lead = jnp.where(
        chip == 0, data, jnp.where(chip == 1, near, jnp.where(chip == 2, side, far))
    )
    held = lax.optimization_barrier(
        (lead, *packets, twin, near_twin, side_twin, far_low_twin, far_high_twin)
    )
    lead, packets = held[0], [packet] + list(held[1:layers][::-1])
    twin, near_twin, side_twin, far_low_twin, far_high_twin = held[layers:]
    halo = lax.ppermute(lead, "sens", [(i + GROUP, i) for i in range(devices - GROUP)])
    halo_twin = flip(halo, 1)
    pieces = [
        data, near, side, twin, near_twin, side_twin,
        far_low, far_high, far_low_twin, far_high_twin,
    ]
    core = inner % 2
    starts = [share * (inner ^ r) for r in (0, 2, 4, 1, 3, 5)]
    starts += [share * (inner ^ 6), share * (inner ^ 6) + half]
    starts += [share * (inner ^ 7), share * (inner ^ 7) + half]
    place = jnp.stack(starts).astype(jnp.int32)
    halo_place = jnp.stack([share * core, share * (1 - core)]).astype(jnp.int32)
    early = early_tables(place, pieces, block, length)
    tables = late_tables(halo_place, [halo, halo_twin], early, block, length)
    gain = math.sqrt(length / chan_count) / length

    def stacks_of(relations):
        chosen = jnp.stack([packets[q] for q in relations])
        count = len(relations) * per_dev
        wide = chosen[:, :item_rows].astype(jnp.float32).reshape(count, 2 * chan_count, LANES)
        ids = chosen[:, item_rows : item_rows + 2 * id_rows].astype(jnp.int32)
        sensor = (ids[:, :id_rows] * sensors_per_group + ids[:, id_rows:]).reshape(-1)
        power = jnp.sum((wide * wide).reshape(count, chan_count, length), axis=2)
        scale = (gain * lax.rsqrt(power / length + EPSILON)).reshape(-1)
        return matched_stacks(sensor, scale, wide, tables, per_dev, lag_rows)

    far_parts = stacks_of(range(layers // 2, layers))
    received = [flip(far_parts[q - layers // 2], GROUP * q) for q in range(layers // 2, layers)]
    near_parts = [stacks_of([q])[0] for q in range(layers // 2)]
    received = [
        near_parts[q] if q == 0 else flip(near_parts[q], GROUP * q) for q in range(layers // 2)
    ] + received
    ordered = []
    for slot in range(layers):
        value = received[slot]
        for mine in range(1, layers):
            value = jnp.where(layer == mine, received[slot ^ mine], value)
        ordered.append(value.reshape(per_dev, block))
    return jnp.concatenate(ordered, axis=1)[:, :lag_count]


def solution(mesh):
    placed = (P(("parts", "sens"), None), P("sens", None, None), P("sens", None), P("sens", None))
    return jax.shard_map(
        body, mesh=mesh, in_specs=placed, out_specs=P(("parts", "sens"), None), check_vma=False
    )
```

```python
import math

import jax
import jax.numpy as jnp
from jax import lax
from jax.experimental import pallas as pl
from jax.experimental.pallas import tpu as pltpu
from jax.sharding import PartitionSpec as P

EPSILON = 1e-05
LANES = 128
HALF = 64
ROWS = 16
GROUP = 8
SLOTS = 4
VMEM_LIMIT = 14 * 2**20
STAGE_ROWS = 33


def start_strip_copies(place, pieces, slab, sem, strip, slot):
    cols = pl.ds(pl.multiple_of(strip * LANES, LANES), LANES)
    made = []
    for i, piece in enumerate(pieces):
        rows = pl.ds(pl.multiple_of(place[i], 16), piece.shape[0])
        made.append(pltpu.make_async_copy(piece.at[:, cols], slab.at[slot, rows], sem.at[slot, i]))
    return made


def for_each_strip(place, pieces, slab, sem, work):
    strips = pieces[0].shape[1] // LANES
    for ahead in range(SLOTS - 1):
        for copy in start_strip_copies(place, pieces, slab, sem, ahead, ahead):
            copy.start()

    def step(strip, carry):
        slot = lax.rem(strip, SLOTS)
        coming = strip + SLOTS - 1

        @pl.when(coming < strips)
        def _():
            for copy in start_strip_copies(place, pieces, slab, sem, coming, lax.rem(coming, SLOTS)):
                copy.start()

        for copy in start_strip_copies(place, pieces, slab, sem, strip, slot):
            copy.wait()
        work(strip, slot)
        return carry

    lax.fori_loop(0, strips, step, 0)


def windowed(source, target, offsets, count):
    for start in range(0, count, HALF):
        value = source[start : start + HALF, :]
        for offset in offsets:
            value = value + source[start + offset : start + offset + HALF, :]
        target[start : start + HALF, :] = value


def table_part(strip, samples, stage, fa, fb, w_ref, g_ref, span, norms, rows, lag_rows, length):
    double = 2 * ROWS
    norm_rows = lag_rows + 3
    origin, limit = span
    first, last = rows
    for index in range(origin, limit):
        value = samples(index)
        at = HALF * (index - origin)
        fa[at : at + HALF, :] = value * value * 0.5
    for parity in range(2):
        for q in range(first, last):
            index = 2 * q + parity
            tile = jnp.concatenate([samples(index), samples(index + length // HALF)], axis=0)
            stage[pl.ds(ROWS * parity + q, LANES, stride=STAGE_ROWS), :] = tile.T
    base = pl.multiple_of(strip * LANES * double, LANES * double)
    top = min(ROWS, -(-last // 8) * 8)
    for item in range(LANES):
        for parity in range(2):
            low = ROWS * parity
            value = stage[STAGE_ROWS * item + low + first : STAGE_ROWS * item + low + top, :]
            target = pl.ds(base + double * item + low + first, top - first)
            w_ref[target, :] = value.astype(jnp.bfloat16)
    count = HALF * (limit - origin)
    windowed(fa, fb, (1, 2, 3), count)
    windowed(fb, fa, (4,), count)
    windowed(fa, fb, (8, 16, 24), count)
    windowed(fb, fa, (32, 64, 96), count - LANES)
    for index in range(*norms):
        at = HALF * (index - origin)
        energy_half = fa[at : at + HALF, :] + fa[at + LANES : at + LANES + HALF, :]
        fb[at : at + HALF, :] = lax.rsqrt(energy_half * (2.0 / length) + EPSILON)

    def norm_block(index):
        if norms[0] <= index < norms[1]:
            return fb[HALF * (index - origin) : HALF * (index - origin + 1), :]
        return jnp.zeros((HALF, LANES), jnp.float32)

    base = strip * (LANES * norm_rows)
    for parity in range(2):
        for q in range(first, min(last, lag_rows + 1 - parity)):
            pair = (norm_block(2 * q + parity), norm_block(2 * q + parity - 1))
            target = pl.ds(base + 1 + q, LANES, stride=norm_rows)
            g_ref[parity, target, :] = jnp.concatenate(pair, axis=0).T


def clear(stage):
    for start in range(0, LANES * STAGE_ROWS, LANES):
        stage[start : start + LANES, :] = jnp.zeros((LANES, LANES), jnp.float32)


def stack_templates(sensor, scale, x_ref, w_ref, g_ref, o_ref, sc, first, offset, chan_count, lag_rows):
    shift = lax.broadcasted_iota(jnp.int32, (HALF, LANES), 0) + 1
    lane = lax.broadcasted_iota(jnp.int32, (HALF, LANES), 1)
    upper = (lane < HALF) & (lane >= shift)
    zero = jnp.zeros((HALF, LANES), jnp.float32)
    zero_narrow = jnp.zeros((HALF, LANES), jnp.bfloat16)
    low_out = lax.broadcasted_iota(jnp.int32, (lag_rows, LANES), 1) < HALF

    def one(step, carry):
        k = offset + step
        leading = [jnp.zeros((ROWS, LANES), jnp.float32) for _ in range(2)]
        trailing = [jnp.zeros((ROWS, LANES), jnp.float32) for _ in range(2)]
        for c in range(chan_count):
            item = (first + step) * chan_count + c
            factor = scale[item]
            base = sensor[item] * (lag_rows + 3)
            windows = w_ref[pl.ds(pl.multiple_of(sensor[item] * 2 * ROWS, 2 * ROWS), 2 * ROWS), :]
            lead = jnp.broadcast_to(x_ref[k, 2 * c : 2 * c + 1, :], (HALF, LANES))
            tail = jnp.broadcast_to(x_ref[k, 2 * c + 1 : 2 * c + 2, :], (HALF, LANES))
            lead = pltpu.roll(lead, 1, 1, stride=1, stride_axis=0)
            tail = pltpu.roll(tail, 1, 1, stride=1, stride_axis=0)
            t01 = jnp.where(upper, zero, lead).astype(jnp.bfloat16)
            t23 = jnp.where(upper, lead, tail).astype(jnp.bfloat16)
            t4 = jnp.where(upper, tail, zero).astype(jnp.bfloat16)
            taps = jnp.concatenate(
                [
                    jnp.concatenate([t01, t23], axis=1),
                    jnp.concatenate([t4, zero_narrow], axis=1),
                ],
                axis=0,
            )
            corr = lax.dot_general(
                windows, taps, (((1,), (0,)), ((), ())), preferred_element_type=jnp.float32
            )
            for p in range(2):
                part = corr[ROWS * p : ROWS * (p + 1)]
                leading[p] = leading[p] + part[:, :LANES] * g_ref[p, pl.ds(base + 1, ROWS), :] * factor
                trailing[p] = trailing[p] + part[:, LANES:] * g_ref[p, pl.ds(base, ROWS), :] * factor
        for p in range(2):
            sc[p, 0] = leading[p]
            sc[p, 1] = trailing[p]
        w0 = sc[0, 0, 0:lag_rows] + sc[0, 1, 1 : 1 + lag_rows]
        w0_next = sc[0, 0, 1 : 1 + lag_rows] + sc[0, 1, 2 : 2 + lag_rows]
        w1 = sc[1, 0, 0:lag_rows] + sc[1, 1, 1 : 1 + lag_rows]
        o_ref[pl.ds(step * lag_rows, lag_rows), :] = jnp.where(low_out, w0, w0_next) + pltpu.roll(
            w1, HALF, 1
        )
        return carry

    lax.fori_loop(0, o_ref.shape[0] // lag_rows, one, 0, unroll=4)


def in_vmem(value):
    return pltpu.with_memory_space_constraint(value, pltpu.VMEM)


def cost(microseconds):
    return pl.CostEstimate(
        flops=int(microseconds * 1e9), bytes_accessed=int(microseconds * 1e6), transcendentals=0
    )


def early_tables(place, pieces, block, length):
    sensor_count = pieces[0].shape[1]
    strips = sensor_count // LANES
    lag_rows = block // LANES
    local = (block - length) // HALF
    kept = block - HALF * (local - 1)
    piece_count = len(pieces)

    def kernel(place, *refs):
        ins = refs[:piece_count]
        w_ref, g_ref, tail_ref, slab, stage, fa, fb, sem = refs[piece_count:]
        clear(stage)

        def work(strip, slot):
            def samples(index):
                return slab[slot, HALF * index : HALF * (index + 1), :].astype(jnp.float32)

            tail_ref[strip] = slab[slot, block - kept : block, :]
            table_part(
                strip, samples, stage, fa, fb, w_ref, g_ref,
                (0, block // HALF), (0, local), (0, local // 2), lag_rows, length,
            )

        for_each_strip(place, ins, slab, sem, work)

    whole = pl.BlockSpec(memory_space=pltpu.VMEM)
    return pl.pallas_call(
        kernel,
        grid_spec=pltpu.PrefetchScalarGridSpec(
            num_scalar_prefetch=1,
            grid=(),
            in_specs=[pl.BlockSpec(memory_space=pl.ANY)] * piece_count,
            out_specs=(whole, whole, whole),
            scratch_shapes=[
                pltpu.VMEM((SLOTS, block, LANES), jnp.bfloat16),
                pltpu.VMEM((STAGE_ROWS * LANES, LANES), jnp.float32),
                pltpu.VMEM((block + LANES, LANES), jnp.float32),
                pltpu.VMEM((block + LANES, LANES), jnp.float32),
                pltpu.SemaphoreType.DMA((SLOTS, piece_count)),
            ],
        ),
        out_shape=(
            pltpu.VMEM((sensor_count * 2 * ROWS, LANES), jnp.bfloat16),
            pltpu.VMEM((2, sensor_count * (lag_rows + 3) + 8, LANES), jnp.float32),
            pltpu.VMEM((strips, kept, LANES), jnp.bfloat16),
        ),
        compiler_params=pltpu.CompilerParams(vmem_limit_bytes=VMEM_LIMIT),
    )(place, *pieces)


def late_tables(place, pieces, early, block, length):
    lag_rows = block // LANES
    local = (block - length) // HALF
    total = (block + length) // HALF
    inside = block // HALF
    piece_count = len(pieces)

    def kernel(place, tail_ref, w_in, g_in, *refs):
        ins = refs[:piece_count]
        w_ref, g_ref, slab, stage, fa, fb, sem = refs[piece_count:]
        clear(stage)

        def work(strip, slot):
            def samples(index):
                if index < inside:
                    at = HALF * (index - local + 1)
                    return tail_ref[strip, at : at + HALF, :].astype(jnp.float32)
                if index < total:
                    at = HALF * (index - inside)
                    return slab[slot, at : at + HALF, :].astype(jnp.float32)
                return jnp.zeros((HALF, LANES), jnp.float32)

            table_part(
                strip, samples, stage, fa, fb, w_ref, g_ref,
                (local - 1, total), (local - 1, inside), (local // 2, total // 2), lag_rows, length,
            )

        for_each_strip(place, ins, slab, sem, work)

    whole = pl.BlockSpec(memory_space=pltpu.VMEM)
    span = HALF * (total - local + 1)
    return pl.pallas_call(
        kernel,
        grid_spec=pltpu.PrefetchScalarGridSpec(
            num_scalar_prefetch=1,
            grid=(),
            in_specs=[whole, whole, whole] + [pl.BlockSpec(memory_space=pl.ANY)] * piece_count,
            out_specs=(whole, whole),
            scratch_shapes=[
                pltpu.VMEM((SLOTS, 2 * pieces[0].shape[0], LANES), jnp.bfloat16),
                pltpu.VMEM((STAGE_ROWS * LANES, LANES), jnp.float32),
                pltpu.VMEM((span + LANES, LANES), jnp.float32),
                pltpu.VMEM((span + LANES, LANES), jnp.float32),
                pltpu.SemaphoreType.DMA((SLOTS, piece_count)),
            ],
        ),
        out_shape=(
            pltpu.VMEM(early[0].shape, early[0].dtype),
            pltpu.VMEM(early[1].shape, early[1].dtype),
        ),
        input_output_aliases={2: 0, 3: 1},
        compiler_params=pltpu.CompilerParams(vmem_limit_bytes=VMEM_LIMIT),
    )(place, in_vmem(early[2]), in_vmem(early[0]), in_vmem(early[1]), *pieces)


def matched_stacks(sensor, scale, taps, tables, per_dev, lag_rows):
    count, double, _ = taps.shape
    number = count // per_dev

    def kernel(sensor, scale, x_ref, w_ref, g_ref, *refs):
        for i in range(number):
            stack_templates(
                sensor, scale, x_ref, w_ref, g_ref, refs[i], refs[number],
                i * per_dev, i * per_dev, double // 2, lag_rows,
            )

    whole = pl.BlockSpec(memory_space=pltpu.VMEM)
    return pl.pallas_call(
        kernel,
        grid_spec=pltpu.PrefetchScalarGridSpec(
            num_scalar_prefetch=2,
            grid=(),
            in_specs=[whole, whole, whole],
            out_specs=[whole] * number,
            scratch_shapes=[pltpu.VMEM((2, 2, ROWS, LANES), jnp.float32)],
        ),
        out_shape=[jax.ShapeDtypeStruct((per_dev * lag_rows, LANES), jnp.float32)] * number,
        compiler_params=pltpu.CompilerParams(vmem_limit_bytes=VMEM_LIMIT),
        cost_estimate=cost(8 * number),
    )(sensor, scale, taps, in_vmem(tables[0]), in_vmem(tables[1]))


def body(data, templates, cover, channel):
    devices = lax.axis_size("sens")
    layers = devices // GROUP
    per_dev, chan_count, length = templates.shape
    share, sensor_count = data.shape
    sensors_per_group = sensor_count // devices
    block = share * GROUP
    lag_rows = block // LANES
    lag_count = share * devices - length
    half = share // 2
    me = lax.axis_index("sens")
    layer, inner = me // GROUP, me % GROUP

    def flip(value, bits):
        return lax.ppermute(value, "sens", [(i, i ^ bits) for i in range(devices)])

    item_rows = per_dev * 2 * chan_count
    id_rows = per_dev * chan_count // LANES
    reversed_halves = templates.reshape(item_rows, LANES)[:, ::-1]
    pad_rows = -(item_rows + 2 * id_rows) % 16
    packet = jnp.concatenate(
        [
            reversed_halves,
            cover.reshape(id_rows, LANES).astype(jnp.bfloat16),
            channel.reshape(id_rows, LANES).astype(jnp.bfloat16),
            jnp.zeros((pad_rows, LANES), jnp.bfloat16),
        ],
        axis=0,
    )

    near = flip(data, 2)
    side = flip(data, 4)
    across = flip(packet, 2 * GROUP)
    next_door = flip(packet, GROUP)
    twin = flip(data, 1)
    near, side, across = lax.optimization_barrier((near, side, across))
    far_low = flip(near[:half], 4)
    far_high = flip(side[half:], 2)
    near_twin = flip(near, 1)
    side_twin = flip(side, 1)
    far_low_twin = flip(far_low, 1)
    far_high_twin = flip(far_high, 1)
    far = jnp.concatenate([far_low, far_high], axis=0)
    chip = inner // 2
    lead = jnp.where(
        chip == 0, data, jnp.where(chip == 1, near, jnp.where(chip == 2, side, far))
    )
    beyond = flip(across, GROUP)
    lead, across, next_door, beyond, twin, near_twin, side_twin, far_low_twin, far_high_twin = (
        lax.optimization_barrier(
            (lead, across, next_door, beyond, twin, near_twin, side_twin, far_low_twin, far_high_twin)
        )
    )
    packets = [packet, next_door, across, beyond]
    halo = lax.ppermute(lead, "sens", [(i + GROUP, i) for i in range(devices - GROUP)])
    halo_twin = flip(halo, 1)
    pieces = [
        data, near, side, twin, near_twin, side_twin,
        far_low, far_high, far_low_twin, far_high_twin,
    ]
    core = inner % 2
    starts = [share * (inner ^ r) for r in (0, 2, 4, 1, 3, 5)]
    starts += [share * (inner ^ 6), share * (inner ^ 6) + half]
    starts += [share * (inner ^ 7), share * (inner ^ 7) + half]
    place = jnp.stack(starts).astype(jnp.int32)
    halo_place = jnp.stack([share * core, share * (1 - core)]).astype(jnp.int32)
    early = early_tables(place, pieces, block, length)
    tables = late_tables(halo_place, [halo, halo_twin], early, block, length)
    gain = math.sqrt(length / chan_count) / length

    def stacks_of(relations):
        chosen = jnp.stack([packets[q] for q in relations])
        count = len(relations) * per_dev
        wide = chosen[:, :item_rows].astype(jnp.float32).reshape(count, 2 * chan_count, LANES)
        ids = chosen[:, item_rows : item_rows + 2 * id_rows].astype(jnp.int32)
        sensor = (ids[:, :id_rows] * sensors_per_group + ids[:, id_rows:]).reshape(-1)
        power = jnp.sum((wide * wide).reshape(count, chan_count, length), axis=2)
        scale = (gain * lax.rsqrt(power / length + EPSILON)).reshape(-1)
        return matched_stacks(sensor, scale, wide, tables, per_dev, lag_rows)

    far_parts = stacks_of(range(layers // 2, layers))
    received = [flip(far_parts[q - layers // 2], GROUP * q) for q in range(layers // 2, layers)]
    near_parts = [stacks_of([q])[0] for q in range(layers // 2)]
    received = [
        near_parts[q] if q == 0 else flip(near_parts[q], GROUP * q) for q in range(layers // 2)
    ] + received
    ordered = []
    for slot in range(layers):
        value = received[slot]
        for mine in range(1, layers):
            value = jnp.where(layer == mine, received[slot ^ mine], value)
        ordered.append(value.reshape(per_dev, block))
    return jnp.concatenate(ordered, axis=1)[:, :lag_count]


def solution(mesh):
    placed = (P(("parts", "sens"), None), P("sens", None, None), P("sens", None), P("sens", None))
    return jax.shard_map(
        body, mesh=mesh, in_specs=placed, out_specs=P(("parts", "sens"), None), check_vma=False
    )
```

```python
import math

import jax
import jax.numpy as jnp
from jax import lax
from jax.experimental import pallas as pl
from jax.experimental.pallas import tpu as pltpu
from jax.sharding import PartitionSpec as P

EPSILON = 1e-05
LANES = 128
HALF = 64
ROWS = 16
GROUP = 8
SLOTS = 4
VMEM_LIMIT = 14 * 2**20
STAGE_ROWS = 33


def start_strip_copies(place, pieces, slab, sem, strip, slot):
    cols = pl.ds(pl.multiple_of(strip * LANES, LANES), LANES)
    made = []
    for i, piece in enumerate(pieces):
        rows = pl.ds(pl.multiple_of(place[i], 16), piece.shape[0])
        made.append(pltpu.make_async_copy(piece.at[:, cols], slab.at[slot, rows], sem.at[slot, i]))
    return made


def for_each_strip(place, pieces, slab, sem, work):
    strips = pieces[0].shape[1] // LANES
    for ahead in range(SLOTS - 1):
        for copy in start_strip_copies(place, pieces, slab, sem, ahead, ahead):
            copy.start()

    def step(strip, carry):
        slot = lax.rem(strip, SLOTS)
        coming = strip + SLOTS - 1

        @pl.when(coming < strips)
        def _():
            for copy in start_strip_copies(place, pieces, slab, sem, coming, lax.rem(coming, SLOTS)):
                copy.start()

        for copy in start_strip_copies(place, pieces, slab, sem, strip, slot):
            copy.wait()
        work(strip, slot)
        return carry

    lax.fori_loop(0, strips, step, 0)


def windowed(source, target, offsets, count):
    for start in range(0, count, HALF):
        value = source[start : start + HALF, :]
        for offset in offsets:
            value = value + source[start + offset : start + offset + HALF, :]
        target[start : start + HALF, :] = value


def table_part(strip, samples, stage, fa, fb, w_ref, g_ref, span, norms, rows, lag_rows, length):
    double = 2 * ROWS
    norm_rows = lag_rows + 3
    origin, limit = span
    first, last = rows
    for index in range(origin, limit):
        value = samples(index)
        at = HALF * (index - origin)
        fa[at : at + HALF, :] = value * value * 0.5
    for parity in range(2):
        for q in range(first, last):
            index = 2 * q + parity
            tile = jnp.concatenate([samples(index), samples(index + length // HALF)], axis=0)
            stage[pl.ds(ROWS * parity + q, LANES, stride=STAGE_ROWS), :] = tile.T
    base = pl.multiple_of(strip * LANES * double, LANES * double)
    top = min(ROWS, -(-last // 8) * 8)
    for item in range(LANES):
        for parity in range(2):
            low = ROWS * parity
            value = stage[STAGE_ROWS * item + low + first : STAGE_ROWS * item + low + top, :]
            target = pl.ds(base + double * item + low + first, top - first)
            w_ref[target, :] = value.astype(jnp.bfloat16)
    count = HALF * (limit - origin)
    windowed(fa, fb, (1, 2, 3), count)
    windowed(fb, fa, (4,), count)
    windowed(fa, fb, (8, 16, 24), count)
    windowed(fb, fa, (32, 64, 96), count - LANES)
    for index in range(*norms):
        at = HALF * (index - origin)
        energy_half = fa[at : at + HALF, :] + fa[at + LANES : at + LANES + HALF, :]
        fb[at : at + HALF, :] = lax.rsqrt(energy_half * (2.0 / length) + EPSILON)

    def norm_block(index):
        if norms[0] <= index < norms[1]:
            return fb[HALF * (index - origin) : HALF * (index - origin + 1), :]
        return jnp.zeros((HALF, LANES), jnp.float32)

    base = strip * (LANES * norm_rows)
    for parity in range(2):
        for q in range(first, min(last, lag_rows + 1 - parity)):
            pair = (norm_block(2 * q + parity), norm_block(2 * q + parity - 1))
            target = pl.ds(base + 1 + q, LANES, stride=norm_rows)
            g_ref[parity, target, :] = jnp.concatenate(pair, axis=0).T


def clear(stage):
    for start in range(0, LANES * STAGE_ROWS, LANES):
        stage[start : start + LANES, :] = jnp.zeros((LANES, LANES), jnp.float32)


def stack_templates(sensor, scale, x_ref, w_ref, g_ref, o_ref, sc, first, offset, chan_count, lag_rows):
    shift = lax.broadcasted_iota(jnp.int32, (HALF, LANES), 0) + 1
    lane = lax.broadcasted_iota(jnp.int32, (HALF, LANES), 1)
    upper = (lane < HALF) & (lane >= shift)
    zero = jnp.zeros((HALF, LANES), jnp.float32)
    zero_narrow = jnp.zeros((HALF, LANES), jnp.bfloat16)
    low_out = lax.broadcasted_iota(jnp.int32, (lag_rows, LANES), 1) < HALF

    def one(step, carry):
        k = offset + step
        leading = [jnp.zeros((ROWS, LANES), jnp.float32) for _ in range(2)]
        trailing = [jnp.zeros((ROWS, LANES), jnp.float32) for _ in range(2)]
        for c in range(chan_count):
            item = (first + step) * chan_count + c
            factor = scale[item]
            base = sensor[item] * (lag_rows + 3)
            windows = w_ref[pl.ds(pl.multiple_of(sensor[item] * 2 * ROWS, 2 * ROWS), 2 * ROWS), :]
            lead = jnp.broadcast_to(x_ref[k, 2 * c : 2 * c + 1, :], (HALF, LANES))
            tail = jnp.broadcast_to(x_ref[k, 2 * c + 1 : 2 * c + 2, :], (HALF, LANES))
            lead = pltpu.roll(lead, 1, 1, stride=1, stride_axis=0)
            tail = pltpu.roll(tail, 1, 1, stride=1, stride_axis=0)
            t01 = jnp.where(upper, zero, lead).astype(jnp.bfloat16)
            t23 = jnp.where(upper, lead, tail).astype(jnp.bfloat16)
            t4 = jnp.where(upper, tail, zero).astype(jnp.bfloat16)
            taps = jnp.concatenate(
                [
                    jnp.concatenate([t01, t23], axis=1),
                    jnp.concatenate([t4, zero_narrow], axis=1),
                ],
                axis=0,
            )
            corr = lax.dot_general(
                windows, taps, (((1,), (0,)), ((), ())), preferred_element_type=jnp.float32
            )
            for p in range(2):
                part = corr[ROWS * p : ROWS * (p + 1)]
                leading[p] = leading[p] + part[:, :LANES] * g_ref[p, pl.ds(base + 1, ROWS), :] * factor
                trailing[p] = trailing[p] + part[:, LANES:] * g_ref[p, pl.ds(base, ROWS), :] * factor
        for p in range(2):
            sc[p, 0] = leading[p]
            sc[p, 1] = trailing[p]
        w0 = sc[0, 0, 0:lag_rows] + sc[0, 1, 1 : 1 + lag_rows]
        w0_next = sc[0, 0, 1 : 1 + lag_rows] + sc[0, 1, 2 : 2 + lag_rows]
        w1 = sc[1, 0, 0:lag_rows] + sc[1, 1, 1 : 1 + lag_rows]
        o_ref[pl.ds(step * lag_rows, lag_rows), :] = jnp.where(low_out, w0, w0_next) + pltpu.roll(
            w1, HALF, 1
        )
        return carry

    lax.fori_loop(0, o_ref.shape[0] // lag_rows, one, 0, unroll=4)


def in_vmem(value):
    return pltpu.with_memory_space_constraint(value, pltpu.VMEM)


def cost(microseconds):
    return pl.CostEstimate(
        flops=int(microseconds * 1e9), bytes_accessed=int(microseconds * 1e6), transcendentals=0
    )


def early_tables(place, pieces, block, length):
    sensor_count = pieces[0].shape[1]
    strips = sensor_count // LANES
    lag_rows = block // LANES
    local = (block - length) // HALF
    kept = block - HALF * (local - 1)
    piece_count = len(pieces)

    def kernel(place, *refs):
        ins = refs[:piece_count]
        w_ref, g_ref, tail_ref, slab, stage, fa, fb, sem = refs[piece_count:]
        clear(stage)

        def work(strip, slot):
            def samples(index):
                return slab[slot, HALF * index : HALF * (index + 1), :].astype(jnp.float32)

            tail_ref[strip] = slab[slot, block - kept : block, :]
            table_part(
                strip, samples, stage, fa, fb, w_ref, g_ref,
                (0, block // HALF), (0, local), (0, local // 2), lag_rows, length,
            )

        for_each_strip(place, ins, slab, sem, work)

    whole = pl.BlockSpec(memory_space=pltpu.VMEM)
    return pl.pallas_call(
        kernel,
        grid_spec=pltpu.PrefetchScalarGridSpec(
            num_scalar_prefetch=1,
            grid=(),
            in_specs=[pl.BlockSpec(memory_space=pl.ANY)] * piece_count,
            out_specs=(whole, whole, whole),
            scratch_shapes=[
                pltpu.VMEM((SLOTS, block, LANES), jnp.bfloat16),
                pltpu.VMEM((STAGE_ROWS * LANES, LANES), jnp.float32),
                pltpu.VMEM((block + LANES, LANES), jnp.float32),
                pltpu.VMEM((block + LANES, LANES), jnp.float32),
                pltpu.SemaphoreType.DMA((SLOTS, piece_count)),
            ],
        ),
        out_shape=(
            pltpu.VMEM((sensor_count * 2 * ROWS, LANES), jnp.bfloat16),
            pltpu.VMEM((2, sensor_count * (lag_rows + 3) + 8, LANES), jnp.float32),
            pltpu.VMEM((strips, kept, LANES), jnp.bfloat16),
        ),
        compiler_params=pltpu.CompilerParams(vmem_limit_bytes=VMEM_LIMIT),
    )(place, *pieces)


def late_tables(place, pieces, early, block, length):
    lag_rows = block // LANES
    local = (block - length) // HALF
    total = (block + length) // HALF
    inside = block // HALF
    piece_count = len(pieces)

    def kernel(place, tail_ref, w_in, g_in, *refs):
        ins = refs[:piece_count]
        w_ref, g_ref, slab, stage, fa, fb, sem = refs[piece_count:]
        clear(stage)

        def work(strip, slot):
            def samples(index):
                if index < inside:
                    at = HALF * (index - local + 1)
                    return tail_ref[strip, at : at + HALF, :].astype(jnp.float32)
                if index < total:
                    at = HALF * (index - inside)
                    return slab[slot, at : at + HALF, :].astype(jnp.float32)
                return jnp.zeros((HALF, LANES), jnp.float32)

            table_part(
                strip, samples, stage, fa, fb, w_ref, g_ref,
                (local - 1, total), (local - 1, inside), (local // 2, total // 2), lag_rows, length,
            )

        for_each_strip(place, ins, slab, sem, work)

    whole = pl.BlockSpec(memory_space=pltpu.VMEM)
    span = HALF * (total - local + 1)
    return pl.pallas_call(
        kernel,
        grid_spec=pltpu.PrefetchScalarGridSpec(
            num_scalar_prefetch=1,
            grid=(),
            in_specs=[whole, whole, whole] + [pl.BlockSpec(memory_space=pl.ANY)] * piece_count,
            out_specs=(whole, whole),
            scratch_shapes=[
                pltpu.VMEM((SLOTS, 2 * pieces[0].shape[0], LANES), jnp.bfloat16),
                pltpu.VMEM((STAGE_ROWS * LANES, LANES), jnp.float32),
                pltpu.VMEM((span + LANES, LANES), jnp.float32),
                pltpu.VMEM((span + LANES, LANES), jnp.float32),
                pltpu.SemaphoreType.DMA((SLOTS, piece_count)),
            ],
        ),
        out_shape=(
            pltpu.VMEM(early[0].shape, early[0].dtype),
            pltpu.VMEM(early[1].shape, early[1].dtype),
        ),
        input_output_aliases={2: 0, 3: 1},
        compiler_params=pltpu.CompilerParams(vmem_limit_bytes=VMEM_LIMIT),
    )(place, in_vmem(early[2]), in_vmem(early[0]), in_vmem(early[1]), *pieces)


def matched_stacks(sensor, scale, taps, tables, per_dev, lag_rows):
    count, double, _ = taps.shape
    number = count // per_dev

    def kernel(sensor, scale, x_ref, w_ref, g_ref, *refs):
        for i in range(number):
            stack_templates(
                sensor, scale, x_ref, w_ref, g_ref, refs[i], refs[number],
                i * per_dev, i * per_dev, double // 2, lag_rows,
            )

    whole = pl.BlockSpec(memory_space=pltpu.VMEM)
    return pl.pallas_call(
        kernel,
        grid_spec=pltpu.PrefetchScalarGridSpec(
            num_scalar_prefetch=2,
            grid=(),
            in_specs=[whole, whole, whole],
            out_specs=[whole] * number,
            scratch_shapes=[pltpu.VMEM((2, 2, ROWS, LANES), jnp.float32)],
        ),
        out_shape=[jax.ShapeDtypeStruct((per_dev * lag_rows, LANES), jnp.float32)] * number,
        compiler_params=pltpu.CompilerParams(vmem_limit_bytes=VMEM_LIMIT),
        cost_estimate=cost(8 * number),
    )(sensor, scale, taps, in_vmem(tables[0]), in_vmem(tables[1]))


def body(data, templates, cover, channel):
    devices = lax.axis_size("sens")
    layers = devices // GROUP
    per_dev, chan_count, length = templates.shape
    share, sensor_count = data.shape
    sensors_per_group = sensor_count // devices
    block = share * GROUP
    lag_rows = block // LANES
    lag_count = share * devices - length
    half = share // 2
    me = lax.axis_index("sens")
    layer, inner = me // GROUP, me % GROUP

    def flip(value, bits):
        return lax.ppermute(value, "sens", [(i, i ^ bits) for i in range(devices)])

    item_rows = per_dev * 2 * chan_count
    id_rows = per_dev * chan_count // LANES
    reversed_halves = templates.reshape(item_rows, LANES)[:, ::-1]
    pad_rows = -(item_rows + 2 * id_rows) % 16
    packet = jnp.concatenate(
        [
            reversed_halves,
            cover.reshape(id_rows, LANES).astype(jnp.bfloat16),
            channel.reshape(id_rows, LANES).astype(jnp.bfloat16),
            jnp.zeros((pad_rows, LANES), jnp.bfloat16),
        ],
        axis=0,
    )

    near = flip(data, 2)
    side = flip(data, 4)
    across = flip(packet, 2 * GROUP)
    next_door = flip(packet, GROUP)
    twin = flip(data, 1)
    near_held, side_held, across = lax.optimization_barrier((near, side, across))
    far_low = flip(near[:half], 4)
    far_high = flip(side[half:], 2)
    near_twin = flip(near_held, 1)
    side_twin = flip(side_held, 1)
    far_low_twin = flip(far_low, 1)
    far_high_twin = flip(far_high, 1)
    far = jnp.concatenate([far_low, far_high], axis=0)
    chip = inner // 2
    lead = jnp.where(
        chip == 0, data, jnp.where(chip == 1, near, jnp.where(chip == 2, side, far))
    )
    beyond = flip(across, GROUP)
    lead, across, next_door, beyond, twin, near_twin, side_twin, far_low_twin, far_high_twin = (
        lax.optimization_barrier(
            (lead, across, next_door, beyond, twin, near_twin, side_twin, far_low_twin, far_high_twin)
        )
    )
    packets = [packet, next_door, across, beyond]
    halo = lax.ppermute(lead, "sens", [(i + GROUP, i) for i in range(devices - GROUP)])
    halo_twin = flip(halo, 1)
    pieces = [
        data, near, side, twin, near_twin, side_twin,
        far_low, far_high, far_low_twin, far_high_twin,
    ]
    core = inner % 2
    starts = [share * (inner ^ r) for r in (0, 2, 4, 1, 3, 5)]
    starts += [share * (inner ^ 6), share * (inner ^ 6) + half]
    starts += [share * (inner ^ 7), share * (inner ^ 7) + half]
    place = jnp.stack(starts).astype(jnp.int32)
    halo_place = jnp.stack([share * core, share * (1 - core)]).astype(jnp.int32)
    early = early_tables(place, pieces, block, length)
    tables = late_tables(halo_place, [halo, halo_twin], early, block, length)
    gain = math.sqrt(length / chan_count) / length

    def stacks_of(relations):
        chosen = jnp.stack([packets[q] for q in relations])
        count = len(relations) * per_dev
        wide = chosen[:, :item_rows].astype(jnp.float32).reshape(count, 2 * chan_count, LANES)
        ids = chosen[:, item_rows : item_rows + 2 * id_rows].astype(jnp.int32)
        sensor = (ids[:, :id_rows] * sensors_per_group + ids[:, id_rows:]).reshape(-1)
        power = jnp.sum((wide * wide).reshape(count, chan_count, length), axis=2)
        scale = (gain * lax.rsqrt(power / length + EPSILON)).reshape(-1)
        return matched_stacks(sensor, scale, wide, tables, per_dev, lag_rows)

    far_parts = stacks_of(range(layers // 2, layers))
    received = [flip(far_parts[q - layers // 2], GROUP * q) for q in range(layers // 2, layers)]
    near_parts = [stacks_of([q])[0] for q in range(layers // 2)]
    received = [
        near_parts[q] if q == 0 else flip(near_parts[q], GROUP * q) for q in range(layers // 2)
    ] + received
    ordered = []
    for slot in range(layers):
        value = received[slot]
        for mine in range(1, layers):
            value = jnp.where(layer == mine, received[slot ^ mine], value)
        ordered.append(value.reshape(per_dev, block))
    return jnp.concatenate(ordered, axis=1)[:, :lag_count]


def solution(mesh):
    placed = (P(("parts", "sens"), None), P("sens", None, None), P("sens", None), P("sens", None))
    return jax.shard_map(
        body, mesh=mesh, in_specs=placed, out_specs=P(("parts", "sens"), None), check_vma=False
    )
```

```python
import math

import jax
import jax.numpy as jnp
from jax import lax
from jax.experimental import pallas as pl
from jax.experimental.pallas import tpu as pltpu
from jax.sharding import PartitionSpec as P

EPSILON = 1e-05
LANES = 128
HALF = 64
ROWS = 16
GROUP = 8
SLOTS = 4
VMEM_LIMIT = 14 * 2**20
STAGE_ROWS = 33


def start_strip_copies(place, pieces, slab, sem, strip, slot):
    cols = pl.ds(pl.multiple_of(strip * LANES, LANES), LANES)
    made = []
    for i, piece in enumerate(pieces):
        rows = pl.ds(pl.multiple_of(place[i], 16), piece.shape[0])
        made.append(pltpu.make_async_copy(piece.at[:, cols], slab.at[slot, rows], sem.at[slot, i]))
    return made


def for_each_strip(place, pieces, slab, sem, work):
    strips = pieces[0].shape[1] // LANES
    for ahead in range(SLOTS - 1):
        for copy in start_strip_copies(place, pieces, slab, sem, ahead, ahead):
            copy.start()

    def step(strip, carry):
        slot = lax.rem(strip, SLOTS)
        coming = strip + SLOTS - 1

        @pl.when(coming < strips)
        def _():
            for copy in start_strip_copies(place, pieces, slab, sem, coming, lax.rem(coming, SLOTS)):
                copy.start()

        for copy in start_strip_copies(place, pieces, slab, sem, strip, slot):
            copy.wait()
        work(strip, slot)
        return carry

    lax.fori_loop(0, strips, step, 0)


def windowed(source, target, offsets, count):
    for start in range(0, count, HALF):
        value = source[start : start + HALF, :]
        for offset in offsets:
            value = value + source[start + offset : start + offset + HALF, :]
        target[start : start + HALF, :] = value


def table_part(strip, samples, stage, fa, fb, w_ref, g_ref, span, norms, rows, lag_rows, length):
    double = 2 * ROWS
    norm_rows = lag_rows + 3
    origin, limit = span
    first, last = rows
    for index in range(origin, limit):
        value = samples(index)
        at = HALF * (index - origin)
        fa[at : at + HALF, :] = value * value * 0.5
    for parity in range(2):
        for q in range(first, last):
            index = 2 * q + parity
            tile = jnp.concatenate([samples(index), samples(index + length // HALF)], axis=0)
            stage[pl.ds(ROWS * parity + q, LANES, stride=STAGE_ROWS), :] = tile.T
    base = pl.multiple_of(strip * LANES * double, LANES * double)
    top = min(ROWS, -(-last // 8) * 8)
    for item in range(LANES):
        for parity in range(2):
            low = ROWS * parity
            value = stage[STAGE_ROWS * item + low + first : STAGE_ROWS * item + low + top, :]
            target = pl.ds(base + double * item + low + first, top - first)
            w_ref[target, :] = value.astype(jnp.bfloat16)
    count = HALF * (limit - origin)
    windowed(fa, fb, (1, 2, 3), count)
    windowed(fb, fa, (4,), count)
    windowed(fa, fb, (8, 16, 24), count)
    windowed(fb, fa, (32, 64, 96), count - LANES)
    for index in range(*norms):
        at = HALF * (index - origin)
        energy_half = fa[at : at + HALF, :] + fa[at + LANES : at + LANES + HALF, :]
        fb[at : at + HALF, :] = lax.rsqrt(energy_half * (2.0 / length) + EPSILON)

    def norm_block(index):
        if norms[0] <= index < norms[1]:
            return fb[HALF * (index - origin) : HALF * (index - origin + 1), :]
        return jnp.zeros((HALF, LANES), jnp.float32)

    base = strip * (LANES * norm_rows)
    for parity in range(2):
        for q in range(first, min(last, lag_rows + 1 - parity)):
            pair = (norm_block(2 * q + parity), norm_block(2 * q + parity - 1))
            target = pl.ds(base + 1 + q, LANES, stride=norm_rows)
            g_ref[parity, target, :] = jnp.concatenate(pair, axis=0).T


def clear(stage):
    for start in range(0, LANES * STAGE_ROWS, LANES):
        stage[start : start + LANES, :] = jnp.zeros((LANES, LANES), jnp.float32)


def stack_templates(sensor, scale, x_ref, w_ref, g_ref, o_ref, sc, first, offset, chan_count, lag_rows):
    shift = lax.broadcasted_iota(jnp.int32, (HALF, LANES), 0) + 1
    lane = lax.broadcasted_iota(jnp.int32, (HALF, LANES), 1)
    upper = (lane < HALF) & (lane >= shift)
    zero = jnp.zeros((HALF, LANES), jnp.float32)
    zero_narrow = jnp.zeros((HALF, LANES), jnp.bfloat16)
    low_out = lax.broadcasted_iota(jnp.int32, (lag_rows, LANES), 1) < HALF

    def one(step, carry):
        k = offset + step
        leading = [jnp.zeros((ROWS, LANES), jnp.float32) for _ in range(2)]
        trailing = [jnp.zeros((ROWS, LANES), jnp.float32) for _ in range(2)]
        for c in range(chan_count):
            item = (first + step) * chan_count + c
            factor = scale[item]
            base = sensor[item] * (lag_rows + 3)
            windows = w_ref[pl.ds(pl.multiple_of(sensor[item] * 2 * ROWS, 2 * ROWS), 2 * ROWS), :]
            lead = jnp.broadcast_to(x_ref[k, 2 * c : 2 * c + 1, :], (HALF, LANES))
            tail = jnp.broadcast_to(x_ref[k, 2 * c + 1 : 2 * c + 2, :], (HALF, LANES))
            lead = pltpu.roll(lead, 1, 1, stride=1, stride_axis=0)
            tail = pltpu.roll(tail, 1, 1, stride=1, stride_axis=0)
            t01 = jnp.where(upper, zero, lead).astype(jnp.bfloat16)
            t23 = jnp.where(upper, lead, tail).astype(jnp.bfloat16)
            t4 = jnp.where(upper, tail, zero).astype(jnp.bfloat16)
            taps = jnp.concatenate(
                [
                    jnp.concatenate([t01, t23], axis=1),
                    jnp.concatenate([t4, zero_narrow], axis=1),
                ],
                axis=0,
            )
            corr = lax.dot_general(
                windows, taps, (((1,), (0,)), ((), ())), preferred_element_type=jnp.float32
            )
            for p in range(2):
                part = corr[ROWS * p : ROWS * (p + 1)]
                leading[p] = leading[p] + part[:, :LANES] * g_ref[p, pl.ds(base + 1, ROWS), :] * factor
                trailing[p] = trailing[p] + part[:, LANES:] * g_ref[p, pl.ds(base, ROWS), :] * factor
        for p in range(2):
            sc[p, 0] = leading[p]
            sc[p, 1] = trailing[p]
        w0 = sc[0, 0, 0:lag_rows] + sc[0, 1, 1 : 1 + lag_rows]
        w0_next = sc[0, 0, 1 : 1 + lag_rows] + sc[0, 1, 2 : 2 + lag_rows]
        w1 = sc[1, 0, 0:lag_rows] + sc[1, 1, 1 : 1 + lag_rows]
        o_ref[pl.ds(step * lag_rows, lag_rows), :] = jnp.where(low_out, w0, w0_next) + pltpu.roll(
            w1, HALF, 1
        )
        return carry

    lax.fori_loop(0, o_ref.shape[0] // lag_rows, one, 0, unroll=4)


def in_vmem(value):
    return pltpu.with_memory_space_constraint(value, pltpu.VMEM)


def cost(microseconds):
    return pl.CostEstimate(
        flops=int(microseconds * 1e9), bytes_accessed=int(microseconds * 1e6), transcendentals=0
    )


def early_tables(place, pieces, block, length):
    sensor_count = pieces[0].shape[1]
    strips = sensor_count // LANES
    lag_rows = block // LANES
    local = (block - length) // HALF
    kept = block - HALF * (local - 1)
    piece_count = len(pieces)

    def kernel(place, *refs):
        ins = refs[:piece_count]
        w_ref, g_ref, tail_ref, slab, stage, fa, fb, sem = refs[piece_count:]
        clear(stage)

        def work(strip, slot):
            def samples(index):
                return slab[slot, HALF * index : HALF * (index + 1), :].astype(jnp.float32)

            tail_ref[strip] = slab[slot, block - kept : block, :]
            table_part(
                strip, samples, stage, fa, fb, w_ref, g_ref,
                (0, block // HALF), (0, local), (0, local // 2), lag_rows, length,
            )

        for_each_strip(place, ins, slab, sem, work)

    whole = pl.BlockSpec(memory_space=pltpu.VMEM)
    return pl.pallas_call(
        kernel,
        grid_spec=pltpu.PrefetchScalarGridSpec(
            num_scalar_prefetch=1,
            grid=(),
            in_specs=[pl.BlockSpec(memory_space=pl.ANY)] * piece_count,
            out_specs=(whole, whole, whole),
            scratch_shapes=[
                pltpu.VMEM((SLOTS, block, LANES), jnp.bfloat16),
                pltpu.VMEM((STAGE_ROWS * LANES, LANES), jnp.float32),
                pltpu.VMEM((block + LANES, LANES), jnp.float32),
                pltpu.VMEM((block + LANES, LANES), jnp.float32),
                pltpu.SemaphoreType.DMA((SLOTS, piece_count)),
            ],
        ),
        out_shape=(
            pltpu.VMEM((sensor_count * 2 * ROWS, LANES), jnp.bfloat16),
            pltpu.VMEM((2, sensor_count * (lag_rows + 3) + 8, LANES), jnp.float32),
            pltpu.VMEM((strips, kept, LANES), jnp.bfloat16),
        ),
        compiler_params=pltpu.CompilerParams(vmem_limit_bytes=VMEM_LIMIT),
    )(place, *pieces)


def late_tables(place, pieces, early, block, length):
    lag_rows = block // LANES
    local = (block - length) // HALF
    total = (block + length) // HALF
    inside = block // HALF
    piece_count = len(pieces)

    def kernel(place, tail_ref, w_in, g_in, *refs):
        ins = refs[:piece_count]
        w_ref, g_ref, slab, stage, fa, fb, sem = refs[piece_count:]
        clear(stage)

        def work(strip, slot):
            def samples(index):
                if index < inside:
                    at = HALF * (index - local + 1)
                    return tail_ref[strip, at : at + HALF, :].astype(jnp.float32)
                if index < total:
                    at = HALF * (index - inside)
                    return slab[slot, at : at + HALF, :].astype(jnp.float32)
                return jnp.zeros((HALF, LANES), jnp.float32)

            table_part(
                strip, samples, stage, fa, fb, w_ref, g_ref,
                (local - 1, total), (local - 1, inside), (local // 2, total // 2), lag_rows, length,
            )

        for_each_strip(place, ins, slab, sem, work)

    whole = pl.BlockSpec(memory_space=pltpu.VMEM)
    span = HALF * (total - local + 1)
    return pl.pallas_call(
        kernel,
        grid_spec=pltpu.PrefetchScalarGridSpec(
            num_scalar_prefetch=1,
            grid=(),
            in_specs=[whole, whole, whole] + [pl.BlockSpec(memory_space=pl.ANY)] * piece_count,
            out_specs=(whole, whole),
            scratch_shapes=[
                pltpu.VMEM((SLOTS, 2 * pieces[0].shape[0], LANES), jnp.bfloat16),
                pltpu.VMEM((STAGE_ROWS * LANES, LANES), jnp.float32),
                pltpu.VMEM((span + LANES, LANES), jnp.float32),
                pltpu.VMEM((span + LANES, LANES), jnp.float32),
                pltpu.SemaphoreType.DMA((SLOTS, piece_count)),
            ],
        ),
        out_shape=(
            pltpu.VMEM(early[0].shape, early[0].dtype),
            pltpu.VMEM(early[1].shape, early[1].dtype),
        ),
        input_output_aliases={2: 0, 3: 1},
        compiler_params=pltpu.CompilerParams(vmem_limit_bytes=VMEM_LIMIT),
    )(place, in_vmem(early[2]), in_vmem(early[0]), in_vmem(early[1]), *pieces)


def matched_stacks(sensor, scale, taps, tables, per_dev, lag_rows):
    count, double, _ = taps.shape
    number = count // per_dev

    def kernel(sensor, scale, x_ref, w_ref, g_ref, *refs):
        for i in range(number):
            stack_templates(
                sensor, scale, x_ref, w_ref, g_ref, refs[i], refs[number],
                i * per_dev, i * per_dev, double // 2, lag_rows,
            )

    whole = pl.BlockSpec(memory_space=pltpu.VMEM)
    return pl.pallas_call(
        kernel,
        grid_spec=pltpu.PrefetchScalarGridSpec(
            num_scalar_prefetch=2,
            grid=(),
            in_specs=[whole, whole, whole],
            out_specs=[whole] * number,
            scratch_shapes=[pltpu.VMEM((2, 2, ROWS, LANES), jnp.float32)],
        ),
        out_shape=[jax.ShapeDtypeStruct((per_dev * lag_rows, LANES), jnp.float32)] * number,
        compiler_params=pltpu.CompilerParams(vmem_limit_bytes=VMEM_LIMIT),
        cost_estimate=cost(8 * number),
    )(sensor, scale, taps, in_vmem(tables[0]), in_vmem(tables[1]))


def body(data, templates, cover, channel):
    devices = lax.axis_size("sens")
    layers = devices // GROUP
    per_dev, chan_count, length = templates.shape
    share, sensor_count = data.shape
    sensors_per_group = sensor_count // devices
    block = share * GROUP
    lag_rows = block // LANES
    lag_count = share * devices - length
    half = share // 2
    me = lax.axis_index("sens")
    layer, inner = me // GROUP, me % GROUP

    def flip(value, bits):
        return lax.ppermute(value, "sens", [(i, i ^ bits) for i in range(devices)])

    item_rows = per_dev * 2 * chan_count
    id_rows = per_dev * chan_count // LANES
    reversed_halves = templates.reshape(item_rows, LANES)[:, ::-1]
    pad_rows = -(item_rows + 2 * id_rows) % 16
    packet = jnp.concatenate(
        [
            reversed_halves,
            cover.reshape(id_rows, LANES).astype(jnp.bfloat16),
            channel.reshape(id_rows, LANES).astype(jnp.bfloat16),
            jnp.zeros((pad_rows, LANES), jnp.bfloat16),
        ],
        axis=0,
    )

    near = flip(data, 2)
    side = flip(data, 4)
    across = flip(packet, 2 * GROUP)
    next_door = flip(packet, GROUP)
    twin = flip(data, 1)
    near_held, side_held, across = lax.optimization_barrier((near, side, across))
    far_low = flip(near[:half], 4)
    far_high = flip(side[half:], 2)
    near_twin = flip(near_held, 1)
    side_twin = flip(side_held, 1)
    far_low_twin = flip(far_low, 1)
    far_high_twin = flip(far_high, 1)
    far = jnp.concatenate([far_low, far_high], axis=0)
    chip = inner // 2
    lead = jnp.where(
        chip == 0, data, jnp.where(chip == 1, near, jnp.where(chip == 2, side, far))
    )
    beyond = flip(across, GROUP)
    lead, across, next_door, beyond, twin, near_twin, side_twin, far_low_twin, far_high_twin = (
        lax.optimization_barrier(
            (lead, across, next_door, beyond, twin, near_twin, side_twin, far_low_twin, far_high_twin)
        )
    )
    packets = [packet, next_door, across, beyond]
    halo = lax.ppermute(lead, "sens", [(i + GROUP, i) for i in range(devices - GROUP)])
    halo_twin = flip(halo, 1)
    pieces = [
        data, near, side, twin, near_twin, side_twin,
        far_low, far_high, far_low_twin, far_high_twin,
    ]
    core = inner % 2
    starts = [share * (inner ^ r) for r in (0, 2, 4, 1, 3, 5)]
    starts += [share * (inner ^ 6), share * (inner ^ 6) + half]
    starts += [share * (inner ^ 7), share * (inner ^ 7) + half]
    place = jnp.stack(starts).astype(jnp.int32)
    halo_place = jnp.stack([share * core, share * (1 - core)]).astype(jnp.int32)
    early = early_tables(place, pieces, block, length)
    tables = late_tables(halo_place, [halo, halo_twin], early, block, length)
    gain = math.sqrt(length / chan_count) / length

    def stacks_of(relations):
        chosen = jnp.stack([packets[q] for q in relations])
        count = len(relations) * per_dev
        wide = chosen[:, :item_rows].astype(jnp.float32).reshape(count, 2 * chan_count, LANES)
        ids = chosen[:, item_rows : item_rows + 2 * id_rows].astype(jnp.int32)
        sensor = (ids[:, :id_rows] * sensors_per_group + ids[:, id_rows:]).reshape(-1)
        power = jnp.sum((wide * wide).reshape(count, chan_count, length), axis=2)
        scale = (gain * lax.rsqrt(power / length + EPSILON)).reshape(-1)
        return matched_stacks(sensor, scale, wide, tables, per_dev, lag_rows)

    (middle,) = stacks_of([2])
    nearby, farthest = stacks_of([1, 3])
    (own,) = stacks_of([0])
    received = [own, flip(nearby, GROUP), flip(middle, 2 * GROUP), flip(farthest, 3 * GROUP)]
    ordered = []
    for slot in range(layers):
        value = received[slot]
        for mine in range(1, layers):
            value = jnp.where(layer == mine, received[slot ^ mine], value)
        ordered.append(value.reshape(per_dev, block))
    return jnp.concatenate(ordered, axis=1)[:, :lag_count]


def solution(mesh):
    placed = (P(("parts", "sens"), None), P("sens", None, None), P("sens", None), P("sens", None))
    return jax.shard_map(
        body, mesh=mesh, in_specs=placed, out_specs=P(("parts", "sens"), None), check_vma=False
    )
```
